128 devices in a mesh: tm: 16 (over z, y), member: 8 (over x, core).
Axes of the slice: x: 4, y: 4, z: 4, core: 2. Of those that a mesh axis runs over, the one named last changes fastest.
Arguments:
- queries: bfloat16 [65536, 512], P(('member', 'tm')), parts along dimension 0, may hold values from -12 to 12
- key_rows: bfloat16 [65536, 512], P(('member', 'tm')), parts along dimension 0, may hold values from -6 to 6
- value_rows: bfloat16 [65536, 512], P(('member', 'tm')), parts along dimension 0, may hold values from -6 to 6
- grad_output: bfloat16 [65536, 512], P(('member', 'tm')), parts along dimension 0, may hold values from -6 to 6
- extra_blocks: int32 [128, 16], P('member'), parts along dimension 0, may hold values from -1 to 511, as said below
Outputs:
- mixed_rows: bfloat16 [65536, 512], P(('member', 'tm')), parts along dimension 0
- query_grad: bfloat16 [65536, 512], P(('member', 'tm')), parts along dimension 0
- key_grad: bfloat16 [65536, 512], P(('member', 'tm')), parts along dimension 0
- value_grad: bfloat16 [65536, 512], P(('member', 'tm')), parts along dimension 0
The draws below stay inside these ranges and needn't reach their ends.
There are 8 independent parts, one for each index of `member`. The reference program is written for one: setup_inputs(seed, part) draws one part's arguments, and reference() takes and returns one part's arrays. A program takes and returns all parts, laid end to end along the dimension named above; each array names one. Nothing has to cross between parts.
Inputs may be any that keep to these rules, and one draw needn't show every extreme that they name: `extra_blocks`: row b lists distinct sub-blocks of 16 rows, each inside an earlier block; -1 marks an empty entry, and empty entries stand after the others. From any one block a row takes either no sub-block or exactly 2.
All inputs are finite; a program needn't handle non-finite values.
Results may differ from the reference program's by a relative error of at most 0.035.
Values may be sent and summed in bfloat16 or wider, within the bound.
A program may use at most 128 MiB of HBM per device.

```python
import math
import jax
import jax.numpy as jnp
from jax import lax

H = 8
HD = 64
HG = 2
BLK = 512
SUB = 16
EXTRA = 16
CAP = 2
D = 512
SEQ = 8192
N_TM = 16


def draw_queries(key, part):
    return jnp.clip(2.0 * jax.random.normal(jax.random.fold_in(key, 1), (SEQ, H * HD), jnp.float32), -12.0, 12.0).astype(jnp.bfloat16)


def draw_key_rows(key, part):
    return jnp.clip(jax.random.normal(jax.random.fold_in(key, 2), (SEQ, H * HD), jnp.float32), -6.0, 6.0).astype(jnp.bfloat16)


def draw_extra_blocks(key, part):
    block_count = N_TM
    per_block = BLK // SUB
    owners_each = EXTRA // CAP
    block_ids = jnp.arange(block_count, dtype=jnp.int32)
    block_gap = block_ids[:, None] - block_ids[None, :]
    usable = block_gap > 0
    last_row = block_ids[:, None] == block_count - 1
    second_row = block_ids[:, None] == block_count - 2
    forced = last_row & ((block_ids[None, :] == block_count - 2) | (block_ids[None, :] == 0)) | second_row & (block_ids[None, :] == block_count // 2 - 2)
    hot_key, score_key, inside_key = jax.random.split(jax.random.fold_in(key, 3), 3)
    popular = jax.random.randint(hot_key, (block_count,), 0, 4) == 0
    raw_scores = jax.random.randint(score_key, (block_count, block_count), 0, 1000) + 1500 * popular.astype(jnp.int32)[None, :] + 100000 * forced.astype(jnp.int32)
    ranked = jnp.where(usable, raw_scores * block_count + block_ids[None, :], -1 - block_ids[None, :])
    top_scores, owners = lax.top_k(ranked, owners_each)
    picked = top_scores >= 0
    inside_scores = jax.random.randint(inside_key, (block_count, owners_each, per_block), 0, 65536) * per_block + jnp.arange(per_block, dtype=jnp.int32)
    inside_top, inside = lax.top_k(inside_scores, CAP)
    entries = owners[:, :, None] * per_block + inside
    entries = jnp.where(picked[:, :, None], entries, -1)
    return entries.reshape(block_count, EXTRA).astype(jnp.int32)


def levels(stream_key, shape, shards, low, top_value):
    level, own = 1.0, jax.random.fold_in(stream_key, 6)
    for position, blocks in shards:
        draws = jnp.exp(jax.random.uniform(jax.random.fold_in(own, position), (blocks,), jnp.float32, low / len(shards), top_value / len(shards)))
        level = level * jnp.repeat(draws, shape[position] // blocks).reshape([-1 if axis == position else 1 for axis in range(len(shape))])
    return level


def centred(key, dims, spread, bound, cuts=(), kind=jnp.bfloat16):
    loudness = levels(key, dims, cuts, -0.22, 0.18) if cuts else 1.0
    result = jax.random.normal(key, dims, jnp.float32) * spread * loudness
    return jnp.minimum(jnp.maximum(result, -bound), bound).astype(kind)


def setup_inputs(seed: int = 0, part: int = 0) -> dict:
    splits = jax.random.split(jax.random.key(seed), 6)
    part_keys = jax.random.split(jax.random.fold_in(splits[5], part), 6)
    return {
        "queries": draw_queries(jax.random.fold_in(jax.random.fold_in(splits[5], part), 71), part),
        "key_rows": draw_key_rows(jax.random.fold_in(jax.random.fold_in(splits[5], part), 71), part),
        "value_rows": centred(part_keys[2], (SEQ, D), 1.0, 6.0, ((0, 16),)),
        "grad_output": centred(part_keys[3], (SEQ, D), 1.0, 6.0, ((0, 16),)),
        "extra_blocks": draw_extra_blocks(jax.random.fold_in(jax.random.fold_in(splits[5], part), 71), part),
    }


very_negative = -1e+30

def rounded(values):
    return lax.optimization_barrier(values.astype(jnp.bfloat16)).astype(jnp.float32)

def split_heads(values):
    return values.reshape(values.shape[0], values.shape[1] // HD, HD).astype(jnp.float32)

def forward_group(query_part, key_part, value_part, key_mask, scaling):
    scores = jnp.einsum('qhd,khd->hqk', split_heads(query_part), split_heads(key_part)) * scaling
    scores = jnp.where(key_mask[None], scores, very_negative)
    weights = jax.nn.softmax(scores, axis=-1)
    weights_low = weights.astype(jnp.bfloat16)
    mixed_heads = jnp.einsum('hqk,khd->qhd', weights_low.astype(jnp.float32), split_heads(value_part))
    mixed_part = mixed_heads.reshape(query_part.shape).astype(jnp.bfloat16)
    return (weights, weights_low, mixed_part)

def backward_group(query_part, key_part, value_part, grad_part, mixed_part, weights, weights_low, scaling):
    grad_heads = split_heads(grad_part)
    row_delta = lax.optimization_barrier(jnp.sum(grad_heads * split_heads(mixed_part), axis=-1))
    row_delta = jnp.transpose(row_delta)[:, :, None]
    weight_grads = jnp.einsum('qhd,khd->hqk', grad_heads, split_heads(value_part))
    score_grads = (weights * (weight_grads - row_delta)).astype(jnp.bfloat16).astype(jnp.float32)
    query_grads = jnp.einsum('hqk,khd->qhd', score_grads, split_heads(key_part)) * scaling
    key_grads = jnp.einsum('hqk,qhd->khd', score_grads, split_heads(query_part)) * scaling
    value_grads = jnp.einsum('hqk,qhd->khd', weights_low.astype(jnp.float32), grad_heads)
    return (query_grads.reshape(query_part.shape), key_grads.reshape(key_part.shape), value_grads.reshape(key_part.shape))

def reference(queries, key_rows, value_rows, grad_output, extra_blocks):
    model_width = queries.shape[1]
    group_width = HG * HD
    group_count = model_width // group_width
    scaling = 1.0 / math.sqrt(HD)
    distances = []
    reach = 1
    while reach < N_TM:
        distances.append(reach)
        reach = reach * 2
    row_ids = jnp.arange(BLK, dtype=jnp.int32)
    own_mask = row_ids[:, None] >= row_ids[None, :]
    key_table = key_rows.reshape(SEQ // SUB, SUB * model_width)
    value_table = value_rows.reshape(SEQ // SUB, SUB * model_width)

    def one_block(accumulated, block_index):
        key_acc, value_acc = accumulated
        row_start = (block_index * BLK).astype(jnp.int32)
        query_block = lax.dynamic_slice_in_dim(queries, row_start, BLK, 0)
        grad_block = lax.dynamic_slice_in_dim(grad_output, row_start, BLK, 0)
        key_list = [lax.dynamic_slice_in_dim(key_rows, row_start, BLK, 0)]
        value_list = [lax.dynamic_slice_in_dim(value_rows, row_start, BLK, 0)]
        live_list = []
        other_starts = []
        for distance in distances:
            other_start = (jnp.maximum(block_index - distance, 0) * BLK).astype(jnp.int32)
            other_starts.append(other_start)
            key_list.append(lax.dynamic_slice_in_dim(key_rows, other_start, BLK, 0))
            value_list.append(lax.dynamic_slice_in_dim(value_rows, other_start, BLK, 0))
            live_list.append(jnp.broadcast_to(block_index >= distance, (BLK,)))
        entries = lax.dynamic_index_in_dim(extra_blocks, block_index, 0, keepdims=False)
        entry_live = entries >= 0
        entry_index = jnp.where(entry_live, entries, 0).astype(jnp.int32)
        key_list.append(jnp.take(key_table, entry_index, axis=0).reshape(EXTRA * SUB, model_width))
        value_list.append(jnp.take(value_table, entry_index, axis=0).reshape(EXTRA * SUB, model_width))
        live_list.append(jnp.repeat(entry_live, SUB))
        far_live = jnp.concatenate(live_list)
        key_mask = jnp.concatenate([own_mask, jnp.broadcast_to(far_live[None, :], (BLK, far_live.shape[0]))], axis=1)
        all_keys = jnp.concatenate(key_list, axis=0)
        all_values = jnp.concatenate(value_list, axis=0)
        mixed_parts, query_parts, key_parts, value_parts = ([], [], [], [])
        for group_index in range(group_count):
            low = group_index * group_width
            high = low + group_width
            weights, weights_low, mixed_part = forward_group(query_block[:, low:high], all_keys[:, low:high], all_values[:, low:high], key_mask, scaling)
            grads = backward_group(query_block[:, low:high], all_keys[:, low:high], all_values[:, low:high], grad_block[:, low:high], mixed_part, weights, weights_low, scaling)
            mixed_parts.append(mixed_part)
            query_parts.append(grads[0])
            key_parts.append(grads[1])
            value_parts.append(grads[2])
        mixed_block = jnp.concatenate(mixed_parts, axis=1)
        query_block_grad = jnp.concatenate(query_parts, axis=1).astype(jnp.bfloat16)
        key_grads = jnp.concatenate(key_parts, axis=1)
        value_grads = jnp.concatenate(value_parts, axis=1)
        key_acc = lax.dynamic_update_slice_in_dim(key_acc, lax.dynamic_slice_in_dim(key_acc, row_start, BLK, 0) + key_grads[:BLK], row_start, 0)
        value_acc = lax.dynamic_update_slice_in_dim(value_acc, lax.dynamic_slice_in_dim(value_acc, row_start, BLK, 0) + value_grads[:BLK], row_start, 0)
        for level, other_start in enumerate(other_starts):
            low = (1 + level) * BLK
            key_term = rounded(key_grads[low:low + BLK])
            value_term = rounded(value_grads[low:low + BLK])
            key_acc = lax.dynamic_update_slice_in_dim(key_acc, lax.dynamic_slice_in_dim(key_acc, other_start, BLK, 0) + key_term, other_start, 0)
            value_acc = lax.dynamic_update_slice_in_dim(value_acc, lax.dynamic_slice_in_dim(value_acc, other_start, BLK, 0) + value_term, other_start, 0)
        extra_start = (1 + len(distances)) * BLK
        key_term = rounded(key_grads[extra_start:]).reshape(EXTRA, SUB * model_width)
        value_term = rounded(value_grads[extra_start:]).reshape(EXTRA, SUB * model_width)
        key_acc = key_acc.reshape(SEQ // SUB, SUB * model_width).at[entry_index].add(key_term).reshape(SEQ, model_width)
        value_acc = value_acc.reshape(SEQ // SUB, SUB * model_width).at[entry_index].add(value_term).reshape(SEQ, model_width)
        return ((key_acc, value_acc), (mixed_block, query_block_grad))
    start_acc = (jnp.zeros((SEQ, model_width), jnp.float32), jnp.zeros((SEQ, model_width), jnp.float32))
    final_acc, outputs = lax.scan(one_block, start_acc, jnp.arange(N_TM, dtype=jnp.int32))
    mixed_rows = outputs[0].reshape(SEQ, model_width)
    query_grad = outputs[1].reshape(SEQ, model_width)
    return (mixed_rows, query_grad, final_acc[0].astype(jnp.bfloat16), final_acc[1].astype(jnp.bfloat16))
```

```python
import math

import jax
import jax.numpy as jnp
from jax import lax
from jax.experimental import pallas as pl
from jax.experimental.pallas import tpu as pltpu
from jax.sharding import PartitionSpec as P

HD = 64
SUB = 16
CAP = 2
MESH = pl.DeviceIdType.MESH
NT = (((1,), (1,)), ((), ()))
NN = (((1,), (0,)), ((), ()))
TN = (((0,), (0,)), ((), ()))
very_negative = -1e30
f32 = jnp.float32
bf16 = jnp.bfloat16

DEVICES = 16
SIDE = 4
BLOCK = 512
WIDTH = 512
PAIR = 128
GROUPS = WIDTH // PAIR
PER_BLOCK = BLOCK // SUB
DISTANCES = (1, 2, 4, 8)
FAR = tuple(d for d in range(1, DEVICES) if d not in DISTANCES)
SLOT_ROWS = CAP * SUB
EXTRA_ROWS = 384
KEYS = 5 * BLOCK + EXTRA_ROWS
CHUNKS = tuple((i * BLOCK, BLOCK) for i in range(5)) + ((5 * BLOCK, EXTRA_ROWS),)


def dot(a, b, dims):
    return lax.dot_general(a, b, dims, preferred_element_type=f32)


def kernel(
    q, k, v, do, table,
    o, dq, dk, dv,
    rx, xx, xs, tb, own, et, xt, rb, cr, xr,
    s_ref, p_ref, vt, qt, dot_t, bias, spread,
    send_kv, recv_kv, send_relay, send_x, recv_x,
    send_t, recv_t, recv_c, send_xt, recv_xt,
):
    me = lax.axis_index("tm")
    col = lax.rem(me, SIDE)
    row = me // SIDE

    def device(index):
        return {"tm": index}

    barrier = pltpu.get_barrier_semaphore()
    for i in range(DEVICES):
        @pl.when(me != i)
        def _():
            pl.semaphore_signal(barrier, inc=1, device_id=device(i), device_id_type=MESH)
    pl.semaphore_wait(barrier, DEVICES - 1)

    def lanes(g):
        return pl.ds(pl.multiple_of(g * PAIR, PAIR), PAIR)

    def kv_copies(g, level, src_k, src_v, send, to):
        return [
            pltpu.make_async_remote_copy(
                src_ref=src,
                dst_ref=rx.at[g, level, part],
                send_sem=send.at[g, level, part],
                recv_sem=recv_kv.at[g, level, part],
                device_id=device(to),
                device_id_type=MESH,
            )
            for part, src in enumerate((src_k, src_v))
        ]

    def own_copies(g, level, to):
        return kv_copies(g, level, k.at[:, lanes(g)], v.at[:, lanes(g)], send_kv, to)

    def relay_copies(g, level, to):
        return kv_copies(g, level, rx.at[g, 2, 0], rx.at[g, 2, 1], send_relay, to)

    direct = (
        (2, me + 4 < DEVICES),
        (0, (col < 3) & (me + 1 < DEVICES)),
        (1, col < 2),
        (3, me + 8 < DEVICES),
    )
    relays = (
        (0, 3, (col == 3) & (row >= 1)),
        (1, 2, (col >= 2) & (row >= 1)),
    )

    def send_blocks(g):
        for level, cond in direct:
            @pl.when(cond)
            def _():
                for copy in own_copies(g, level, me + DISTANCES[level]):
                    copy.start()

    def wait_blocks(g, level):
        @pl.when(me >= DISTANCES[level])
        def _():
            for copy in own_copies(g, level, me):
                copy.wait_recv()

    def relay_blocks(g):
        wait_blocks(g, 2)
        for level, back, cond in relays:
            @pl.when(cond)
            def _():
                for copy in relay_copies(g, level, me - back):
                    copy.start()

    send_blocks(0)
    send_blocks(1)

    def gap_of(i):
        return i + 3 + (i + 10) // 11 + (i + 7) // 11

    def extra_copy(i, to):
        rows = pl.ds(pl.multiple_of(i * SLOT_ROWS, SLOT_ROWS), SLOT_ROWS)
        return pltpu.make_async_remote_copy(
            src_ref=xs.at[:, :, rows, :],
            dst_ref=xx.at[:, :, rows, :],
            send_sem=send_x.at[i],
            recv_sem=recv_x.at[i],
            device_id=device(to),
            device_id_type=MESH,
        )

    spread[...] = jnp.zeros_like(spread)

    def find(i, _):
        other = me + gap_of(i)

        @pl.when(other < DEVICES)
        def _():
            first = me * PER_BLOCK
            count = jnp.int32(0)
            index = [jnp.int32(0), jnp.int32(0)]
            for n in range(table.shape[1]):
                entry = table[other, n]
                inside = entry - first
                mine = (inside >= 0) & (inside < PER_BLOCK)
                for slot in range(CAP):
                    index[slot] = jnp.where(mine & (count == slot), inside, index[slot])
                count = count + jnp.where(mine, 1, 0)
            for slot in range(CAP):
                base = jnp.where(count > slot, index[slot] * SUB, jnp.int32(-4096))
                hit = lax.broadcasted_iota(jnp.int32, (SUB, BLOCK), 1) == (
                    lax.broadcasted_iota(jnp.int32, (SUB, BLOCK), 0) + base
                )
                spread[pl.ds(pl.multiple_of(i * SLOT_ROWS + slot * SUB, SUB), SUB), :] = jnp.where(
                    hit, 1.0, 0.0
                ).astype(bf16)

        return 0

    lax.fori_loop(0, len(FAR), find, 0)
    for part, ref in enumerate((k, v)):
        for g in range(GROUPS):
            xs[g, part] = dot(spread[...], ref[:, g * PAIR:(g + 1) * PAIR], NN).astype(bf16)

    def extras_leave(i, _):
        @pl.when(me + gap_of(i) < DEVICES)
        def _():
            extra_copy(i, me + gap_of(i)).start()
        return 0

    lax.fori_loop(0, len(FAR), extras_leave, 0)

    key_row = lax.broadcasted_iota(jnp.int32, (8, BLOCK), 1)
    for level, distance in enumerate(DISTANCES):
        sub_block = (me - distance) * PER_BLOCK + (key_row >> 4)
        times = jnp.zeros((8, BLOCK), f32)
        for n in range(table.shape[1]):
            times = times + jnp.where(sub_block == table[me, n], 1.0, 0.0)
        value = jnp.where(times > 0.5, 1.0, 0.0)
        low, size = CHUNKS[1 + level]
        bias[:, low:low + size] = jnp.where(sub_block >= 0, value, very_negative)
    key_row = lax.broadcasted_iota(jnp.int32, (8, EXTRA_ROWS), 1)
    place = key_row >> 5
    owner = me - (place + 3 + jnp.where(place >= 1, 1, 0) + jnp.where(place >= 4, 1, 0))
    times = jnp.zeros((8, EXTRA_ROWS), f32)
    for n in range(table.shape[1]):
        entry = table[me, n]
        inside = entry - owner * PER_BLOCK
        times = times + jnp.where((inside >= 0) & (inside < PER_BLOCK), 1.0, 0.0)
    slot_of = ((key_row >> 4) & 1).astype(f32)
    live = (times > slot_of + 0.5) & (owner >= 0) & (place < len(FAR))
    bias[:, 5 * BLOCK:] = jnp.where(live, 0.0, very_negative)

    for level, distance in enumerate(DISTANCES):
        @pl.when(me < distance)
        def _():
            def clear(g, _):
                rx[g, level] = jnp.zeros(rx.shape[2:], bf16)
                return 0
            lax.fori_loop(0, GROUPS, clear, 0)
    tail = len(FAR) * SLOT_ROWS
    xx[:, :, tail:, :] = jnp.zeros((GROUPS, 2, EXTRA_ROWS - tail, PAIR), bf16)
    xr[:, tail:, :] = jnp.zeros((2 * GROUPS, EXTRA_ROWS - tail, PAIR), bf16)

    def clear_extra(i, _):
        rows = pl.ds(pl.multiple_of(i * SLOT_ROWS, SLOT_ROWS), SLOT_ROWS)

        @pl.when(me - gap_of(i) < 0)
        def _():
            xx[:, :, rows, :] = jnp.zeros((GROUPS, 2, SLOT_ROWS, PAIR), bf16)

        @pl.when(me + gap_of(i) >= DEVICES)
        def _():
            xr[:, rows, :] = jnp.zeros((2 * GROUPS, SLOT_ROWS, PAIR), bf16)

        return 0

    lax.fori_loop(0, len(FAR), clear_extra, 0)

    def term_copy(g, level, dst, recv, to):
        return pltpu.make_async_remote_copy(
            src_ref=tb.at[g, level],
            dst_ref=dst,
            send_sem=send_t.at[g, level],
            recv_sem=recv,
            device_id=device(to),
            device_id_type=MESH,
        )

    def term_home(g, level, to):
        return term_copy(g, level, rb.at[g, level], recv_t.at[g, level], to)

    def term_aside(g, level, to):
        return term_copy(g, level, cr.at[g, level], recv_c.at[g, level], to)

    def extra_term(g, i, to):
        rows = pl.ds(pl.multiple_of(i * SLOT_ROWS, SLOT_ROWS), SLOT_ROWS)
        both = pl.ds(2 * g, 2)
        return pltpu.make_async_remote_copy(
            src_ref=xt.at[both, rows, :],
            dst_ref=xr.at[both, rows, :],
            send_sem=send_xt.at[g, i],
            recv_sem=recv_xt.at[g, i],
            device_id=device(to),
            device_id_type=MESH,
        )

    homes = (
        (0, col >= 1),
        (1, col >= 2),
        (3, me >= 8),
        (2, (col < 2) & (row >= 1)),
    )
    asides = (
        (0, 3, (col == 0) & (row >= 1)),
        (1, 2, (col < 2) & (row >= 1)),
    )
    mixes = (
        (0, (col == 3) & (row >= 1)),
        (1, (col >= 2) & (row >= 1)),
    )

    def send_terms(g):
        for part in range(2):
            xt[2 * g + part] = jnp.transpose(et[part]).astype(bf16)
        for level, ahead, cond in asides:
            @pl.when(cond)
            def _():
                term_aside(g, level, me + ahead).start()
        for level, cond in homes:
            @pl.when(cond & (me >= DISTANCES[level]))
            def _():
                term_home(g, level, me - DISTANCES[level]).start()

        def extra(i, _):
            @pl.when(me - gap_of(i) >= 0)
            def _():
                extra_term(g, i, me - gap_of(i)).start()
            return 0

        lax.fori_loop(0, len(FAR), extra, 0)

    def mix_terms(g):
        for level, cond in mixes:
            @pl.when(cond)
            def _():
                term_aside(g, level, me).wait_recv()
                tb[g, 2] = (tb[g, 2].astype(f32) + cr[g, level].astype(f32)).astype(bf16)

        @pl.when((col >= 2) & (row >= 1))
        def _():
            term_home(g, 2, me - 4).start()

    arrivals = (
        (0, (col <= 2) & (me + 1 < DEVICES)),
        (1, col <= 1),
        (2, me + 4 < DEVICES),
        (3, me + 8 < DEVICES),
    )

    def finish(g):
        for level, cond in arrivals:
            @pl.when(cond)
            def _():
                term_home(g, level, me).wait_recv()
                own[g] = own[g] + rb[g, level].astype(f32)

        def extra(i, _):
            @pl.when(me + gap_of(i) < DEVICES)
            def _():
                extra_term(g, i, me).wait_recv()
            return 0

        lax.fori_loop(0, len(FAR), extra, 0)
        for part, ref in enumerate((dk, dv)):
            folded = dot(spread[...], xr[2 * g + part], TN)
            ref[:, lanes(g)] = (jnp.transpose(own[g, part]) + folded).astype(bf16)

    lane = lax.broadcasted_iota(jnp.int32, (BLOCK, PAIR), 1)
    factor = math.log2(math.e) / math.sqrt(HD)
    scaling = 1.0 / math.sqrt(HD)

    def keys_of(g, c, part):
        if c == 0:
            return (k, v)[part][:, lanes(g)]
        if c < 5:
            return rx[g, c - 1, part]
        return xx[g, part]

    def forward(g, head):
        here = (lane // HD) == head
        query = q[:, lanes(g)]
        query = jnp.where(here, query, jnp.zeros_like(query))
        top = jnp.full((BLOCK, PAIR), very_negative, f32)
        for c, (low, size) in enumerate(CHUNKS):
            scores = dot(query, keys_of(g, c, 0), NT) * factor
            if c == 0:
                r = lax.broadcasted_iota(jnp.int32, (BLOCK, BLOCK), 0)
                j = lax.broadcasted_iota(jnp.int32, (BLOCK, BLOCK), 1)
                scores = jnp.where(r >= j, scores, very_negative)
            else:
                scores = scores + bias[0:1, low:low + size]
            s_ref[:, low:low + size] = scores
            for x in range(size // PAIR):
                top = jnp.maximum(top, scores[:, x * PAIR:(x + 1) * PAIR])
        top = jnp.max(top, axis=1, keepdims=True)
        total = jnp.zeros((BLOCK, PAIR), f32)
        mixed = jnp.zeros((HD, BLOCK), f32)
        features = pl.ds(pl.multiple_of(head * HD, HD), HD)
        for c, (low, size) in enumerate(CHUNKS):
            weights = jnp.exp2(s_ref[:, low:low + size] - top)
            for x in range(size // PAIR):
                total = total + weights[:, x * PAIR:(x + 1) * PAIR]
            weights = weights.astype(bf16)
            p_ref[:, low:low + size] = weights
            mixed = mixed + dot(vt[features, low:low + size], weights, NT)
        total = 1.0 / jnp.sum(total, axis=1, keepdims=True)
        mixed = jnp.transpose(mixed)
        mixed = jnp.concatenate([mixed, mixed], axis=1)
        mixed = (mixed * total).astype(bf16)
        grad = do[:, lanes(g)]
        grad = jnp.where(here, grad, jnp.zeros_like(grad)).astype(f32)
        delta = jnp.sum(grad * mixed.astype(f32), axis=1, keepdims=True) * total
        o[:, lanes(g)] = jnp.where(here, mixed, o[:, lanes(g)])
        return (grad * total).astype(bf16), delta

    def backward(g, head, grad, delta):
        here = (lane // HD) == head
        features = pl.ds(pl.multiple_of(head * HD, HD), HD)
        query_t = qt[g, features, :]
        dot_t[...] = jnp.transpose(grad.astype(f32)).astype(bf16)
        grad_t = dot_t[features, :]
        query_grad = jnp.zeros((BLOCK, PAIR), f32)
        for c, (low, size) in enumerate(CHUNKS):
            weight_grads = dot(grad, keys_of(g, c, 1), NT)
            weights = p_ref[:, low:low + size]
            score_grads = (weights.astype(f32) * (weight_grads - delta)).astype(bf16)
            query_grad = query_grad + dot(score_grads, keys_of(g, c, 0), NN)
            key_term = dot(query_t, score_grads, NN) * scaling
            value_term = dot(grad_t, weights, NN)
            for part, term in enumerate((key_term, value_term)):
                if c == 0:
                    own[g, part, features, :] = term
                elif c < 5:
                    tb[g, c - 1, part, features, :] = term.astype(bf16)
                else:
                    et[part, features, :] = term
        query_grad = (query_grad * scaling).astype(bf16)
        dq[:, lanes(g)] = jnp.where(here, query_grad, dq[:, lanes(g)])

    def transposed(a):
        return jnp.transpose(a.astype(f32)).astype(bf16)

    for g in range(GROUPS):
        qt[g] = transposed(q[:, g * PAIR:(g + 1) * PAIR])
    o[...] = jnp.zeros_like(o)
    dq[...] = jnp.zeros_like(dq)

    relay_blocks(0)

    def extras_arrive(i, _):
        @pl.when(me - gap_of(i) >= 0)
        def _():
            extra_copy(i, me).wait_recv()
        return 0

    def step(i, _):
        g = i // 2
        head = i % 2

        @pl.when(head == 0)
        def _():
            for level in (0, 1, 3):
                wait_blocks(g, level)

        @pl.when(i == 0)
        def _():
            lax.fori_loop(0, len(FAR), extras_arrive, 0)

        @pl.when(head == 0)
        def _():
            for c, (low, size) in enumerate(CHUNKS):
                vt[:, low:low + size] = transposed(keys_of(g, c, 1))

        grad, delta = forward(g, head)

        @pl.when((head == 0) & (g + 2 < GROUPS))
        def _():
            send_blocks(g + 2)

        @pl.when((head == 1) & (g + 1 < GROUPS))
        def _():
            relay_blocks(g + 1)

        @pl.when((head == 0) & (g >= 1))
        def _():
            mix_terms(g - 1)

        @pl.when((head == 1) & (g >= 2))
        def _():
            finish(g - 2)

        backward(g, head, grad, delta)

        @pl.when(head == 1)
        def _():
            send_terms(g)

        return 0

    lax.fori_loop(0, 2 * GROUPS, step, 0)
    mix_terms(GROUPS - 1)

    def last(g, _):
        finish(g)
        return 0

    lax.fori_loop(GROUPS - 2, GROUPS, last, 0)

    def extras_left(i, _):
        @pl.when(me + gap_of(i) < DEVICES)
        def _():
            extra_copy(i, me).wait_send()
        return 0

    lax.fori_loop(0, len(FAR), extras_left, 0)

    def left(g, _):
        for level, cond in direct:
            @pl.when(cond)
            def _():
                for copy in own_copies(g, level, me):
                    copy.wait_send()
        for level, back, cond in relays:
            @pl.when(cond)
            def _():
                for copy in relay_copies(g, level, me):
                    copy.wait_send()
        for level, distance in enumerate(DISTANCES):
            @pl.when(me >= distance)
            def _():
                term_home(g, level, me).wait_send()

        def extra(i, _):
            @pl.when(me - gap_of(i) >= 0)
            def _():
                extra_term(g, i, me).wait_send()
            return 0

        lax.fori_loop(0, len(FAR), extra, 0)
        return 0

    lax.fori_loop(0, GROUPS, left, 0)


def local(queries, key_rows, value_rows, grad_output, extra_blocks):
    whole = pl.BlockSpec(memory_space=pltpu.VMEM)
    slots = len(FAR)
    return pl.pallas_call(
        kernel,
        out_shape=[jax.ShapeDtypeStruct((BLOCK, WIDTH), bf16)] * 4,
        in_specs=[whole] * 4 + [pl.BlockSpec(memory_space=pltpu.SMEM)],
        out_specs=[whole] * 4,
        scratch_shapes=[
            pltpu.VMEM((GROUPS, 4, 2, BLOCK, PAIR), bf16),
            pltpu.VMEM((GROUPS, 2, EXTRA_ROWS, PAIR), bf16),
            pltpu.VMEM((GROUPS, 2, EXTRA_ROWS, PAIR), bf16),
            pltpu.VMEM((GROUPS, 4, 2, PAIR, BLOCK), bf16),
            pltpu.VMEM((GROUPS, 2, PAIR, BLOCK), f32),
            pltpu.VMEM((2, PAIR, EXTRA_ROWS), f32),
            pltpu.VMEM((2 * GROUPS, EXTRA_ROWS, PAIR), bf16),
            pltpu.VMEM((GROUPS, 4, 2, PAIR, BLOCK), bf16),
            pltpu.VMEM((GROUPS, 2, 2, PAIR, BLOCK), bf16),
            pltpu.VMEM((2 * GROUPS, EXTRA_ROWS, PAIR), bf16),
            pltpu.VMEM((BLOCK, KEYS), f32),
            pltpu.VMEM((BLOCK, KEYS), bf16),
            pltpu.VMEM((PAIR, KEYS), bf16),
            pltpu.VMEM((GROUPS, PAIR, BLOCK), bf16),
            pltpu.VMEM((PAIR, BLOCK), bf16),
            pltpu.VMEM((8, KEYS), f32),
            pltpu.VMEM((EXTRA_ROWS, BLOCK), bf16),
            pltpu.SemaphoreType.DMA((GROUPS, 4, 2)),
            pltpu.SemaphoreType.DMA((GROUPS, 4, 2)),
            pltpu.SemaphoreType.DMA((GROUPS, 4, 2)),
            pltpu.SemaphoreType.DMA((slots,)),
            pltpu.SemaphoreType.DMA((slots,)),
            pltpu.SemaphoreType.DMA((GROUPS, 4)),
            pltpu.SemaphoreType.DMA((GROUPS, 4)),
            pltpu.SemaphoreType.DMA((GROUPS, 4)),
            pltpu.SemaphoreType.DMA((GROUPS, slots)),
            pltpu.SemaphoreType.DMA((GROUPS, slots)),
        ],
        compiler_params=pltpu.CompilerParams(
            collective_id=0, has_side_effects=True, vmem_limit_bytes=60 << 20
        ),
    )(queries, key_rows, value_rows, grad_output, extra_blocks)


def solution(mesh):
    rows = P(("member", "tm"), None)
    return jax.shard_map(
        local,
        mesh=mesh,
        in_specs=(rows, rows, rows, rows, P("member", None)),
        out_specs=(rows, rows, rows, rows),
        check_vma=False,
    )
```

```python
import math

import jax
import jax.numpy as jnp
from jax import lax
from jax.experimental import pallas as pl
from jax.experimental.pallas import tpu as pltpu
from jax.sharding import PartitionSpec as P

HD = 64
SUB = 16
CAP = 2
MESH = pl.DeviceIdType.MESH
NT = (((1,), (1,)), ((), ()))
NN = (((1,), (0,)), ((), ()))
TN = (((0,), (0,)), ((), ()))
very_negative = -1e30
f32 = jnp.float32
bf16 = jnp.bfloat16

DEVICES = 16
SIDE = 4
BLOCK = 512
WIDTH = 512
PAIR = 128
GROUPS = WIDTH // PAIR
PER_BLOCK = BLOCK // SUB
DISTANCES = (1, 2, 4, 8)
FAR = tuple(d for d in range(1, DEVICES) if d not in DISTANCES)
SLOT_ROWS = CAP * SUB
EXTRA_ROWS = 384
KEYS = 5 * BLOCK + EXTRA_ROWS
CHUNKS = tuple((i * BLOCK, BLOCK) for i in range(5)) + ((5 * BLOCK, EXTRA_ROWS),)


def dot(a, b, dims):
    return lax.dot_general(a, b, dims, preferred_element_type=f32)


def kernel(
    q, k, v, do, table,
    o, dq, dk, dv,
    rx, xx, xs, tb, own, et, xt, rb, cr, xr,
    p_far, p_own, o_own, stats, share_rows, qt, dt, bias, spread,
    send_kv, recv_kv, send_relay, send_x, recv_x,
    send_t, recv_t, recv_c, send_xt, recv_xt,
):
    me = lax.axis_index("tm")
    col = lax.rem(me, SIDE)
    row = me // SIDE

    def device(index):
        return {"tm": index}

    barrier = pltpu.get_barrier_semaphore()
    for i in range(DEVICES):
        @pl.when(me != i)
        def _():
            pl.semaphore_signal(barrier, inc=1, device_id=device(i), device_id_type=MESH)
    pl.semaphore_wait(barrier, DEVICES - 1)

    def lanes(g):
        return pl.ds(pl.multiple_of(g * PAIR, PAIR), PAIR)

    def kv_copies(g, level, src_k, src_v, send, to):
        return [
            pltpu.make_async_remote_copy(
                src_ref=src,
                dst_ref=rx.at[g, level, part],
                send_sem=send.at[g, level, part],
                recv_sem=recv_kv.at[g, level, part],
                device_id=device(to),
                device_id_type=MESH,
            )
            for part, src in enumerate((src_k, src_v))
        ]

    def own_copies(g, level, to):
        return kv_copies(g, level, k.at[:, lanes(g)], v.at[:, lanes(g)], send_kv, to)

    def relay_copies(g, level, to):
        return kv_copies(g, level, rx.at[g, 2, 0], rx.at[g, 2, 1], send_relay, to)

    direct = (
        (2, me + 4 < DEVICES),
        (0, (col < 3) & (me + 1 < DEVICES)),
        (1, col < 2),
        (3, me + 8 < DEVICES),
    )
    relays = (
        (0, 3, (col == 3) & (row >= 1)),
        (1, 2, (col >= 2) & (row >= 1)),
    )

    def send_blocks(g):
        for part in range(2):
            for level, cond in direct:
                @pl.when(cond)
                def _():
                    own_copies(g, level, me + DISTANCES[level])[part].start()

    def wait_blocks(g, level):
        @pl.when(me >= DISTANCES[level])
        def _():
            for copy in own_copies(g, level, me):
                copy.wait_recv()

    def relay_blocks(g):
        wait_blocks(g, 2)
        for level, back, cond in relays:
            @pl.when(cond)
            def _():
                for copy in relay_copies(g, level, me - back):
                    copy.start()

    send_blocks(0)

    def gap_of(i):
        return i + 3 + (i + 10) // 11 + (i + 7) // 11

    def extra_copy(g, i, to):
        rows = pl.ds(pl.multiple_of(i * SLOT_ROWS, SLOT_ROWS), SLOT_ROWS)
        return pltpu.make_async_remote_copy(
            src_ref=xs.at[g, :, rows, :],
            dst_ref=xx.at[g, :, rows, :],
            send_sem=send_x.at[g, i],
            recv_sem=recv_x.at[g, i],
            device_id=device(to),
            device_id_type=MESH,
        )

    spread[...] = jnp.zeros_like(spread)

    def find(i, _):
        other = me + gap_of(i)

        @pl.when(other < DEVICES)
        def _():
            first = me * PER_BLOCK
            count = jnp.int32(0)
            index = [jnp.int32(0), jnp.int32(0)]
            for n in range(table.shape[1]):
                entry = table[other, n]
                inside = entry - first
                mine = (inside >= 0) & (inside < PER_BLOCK)
                for slot in range(CAP):
                    index[slot] = jnp.where(mine & (count == slot), inside, index[slot])
                count = count + jnp.where(mine, 1, 0)
            for slot in range(CAP):
                base = jnp.where(count > slot, index[slot] * SUB, jnp.int32(-4096))
                hit = lax.broadcasted_iota(jnp.int32, (SUB, BLOCK), 1) == (
                    lax.broadcasted_iota(jnp.int32, (SUB, BLOCK), 0) + base
                )
                spread[pl.ds(pl.multiple_of(i * SLOT_ROWS + slot * SUB, SUB), SUB), :] = jnp.where(
                    hit, 1.0, 0.0
                ).astype(bf16)

        return 0

    lax.fori_loop(0, len(FAR), find, 0)
    for part, ref in enumerate((k, v)):
        for g in range(GROUPS):
            xs[g, part] = dot(spread[...], ref[:, g * PAIR:(g + 1) * PAIR], NN).astype(bf16)

    def send_extras(g):
        def one(i, _):
            @pl.when(me + gap_of(i) < DEVICES)
            def _():
                extra_copy(g, i, me + gap_of(i)).start()
            return 0

        lax.fori_loop(0, len(FAR), one, 0)

    relay_blocks(0)
    send_extras(0)

    key_row = lax.broadcasted_iota(jnp.int32, (8, BLOCK), 1)
    for level, distance in enumerate(DISTANCES):
        sub_block = (me - distance) * PER_BLOCK + (key_row >> 4)
        times = jnp.zeros((8, BLOCK), f32)
        for n in range(table.shape[1]):
            times = times + jnp.where(sub_block == table[me, n], 1.0, 0.0)
        value = jnp.where(times > 0.5, 1.0, 0.0)
        low, size = CHUNKS[1 + level]
        bias[:, low:low + size] = jnp.where(sub_block >= 0, value, very_negative)
    key_row = lax.broadcasted_iota(jnp.int32, (8, EXTRA_ROWS), 1)
    place = key_row >> 5
    owner = me - (place + 3 + jnp.where(place >= 1, 1, 0) + jnp.where(place >= 4, 1, 0))
    times = jnp.zeros((8, EXTRA_ROWS), f32)
    for n in range(table.shape[1]):
        entry = table[me, n]
        inside = entry - owner * PER_BLOCK
        times = times + jnp.where((inside >= 0) & (inside < PER_BLOCK), 1.0, 0.0)
    slot_of = ((key_row >> 4) & 1).astype(f32)
    live = (times > slot_of + 0.5) & (owner >= 0) & (place < len(FAR))
    bias[:, 5 * BLOCK:] = jnp.where(live, 0.0, very_negative)

    for level, distance in enumerate(DISTANCES):
        @pl.when(me < distance)
        def _():
            def clear(g, _):
                rx[g, level] = jnp.zeros(rx.shape[2:], bf16)
                return 0
            lax.fori_loop(0, GROUPS, clear, 0)
    tail = len(FAR) * SLOT_ROWS
    xx[:, :, tail:, :] = jnp.zeros((GROUPS, 2, EXTRA_ROWS - tail, PAIR), bf16)
    xr[:, tail:, :] = jnp.zeros((2 * GROUPS, EXTRA_ROWS - tail, PAIR), bf16)

    def clear_extra(i, _):
        rows = pl.ds(pl.multiple_of(i * SLOT_ROWS, SLOT_ROWS), SLOT_ROWS)

        @pl.when(me - gap_of(i) < 0)
        def _():
            xx[:, :, rows, :] = jnp.zeros((GROUPS, 2, SLOT_ROWS, PAIR), bf16)

        @pl.when(me + gap_of(i) >= DEVICES)
        def _():
            xr[:, rows, :] = jnp.zeros((2 * GROUPS, SLOT_ROWS, PAIR), bf16)

        return 0

    lax.fori_loop(0, len(FAR), clear_extra, 0)

    def term_copy(g, level, dst, recv, to):
        return pltpu.make_async_remote_copy(
            src_ref=tb.at[g, level],
            dst_ref=dst,
            send_sem=send_t.at[g, level],
            recv_sem=recv,
            device_id=device(to),
            device_id_type=MESH,
        )

    def term_home(g, level, to):
        return term_copy(g, level, rb.at[g, level], recv_t.at[g, level], to)

    def term_aside(g, level, to):
        return term_copy(g, level, cr.at[g, level], recv_c.at[g, level], to)

    def extra_term(g, i, to):
        rows = pl.ds(pl.multiple_of(i * SLOT_ROWS, SLOT_ROWS), SLOT_ROWS)
        both = pl.ds(2 * g, 2)
        return pltpu.make_async_remote_copy(
            src_ref=xt.at[both, rows, :],
            dst_ref=xr.at[both, rows, :],
            send_sem=send_xt.at[g, i],
            recv_sem=recv_xt.at[g, i],
            device_id=device(to),
            device_id_type=MESH,
        )

    homes = (
        (0, col >= 1),
        (1, col >= 2),
        (3, me >= 8),
        (2, (col < 2) & (row >= 1)),
    )
    asides = (
        (0, 3, (col == 0) & (row >= 1)),
        (1, 2, (col < 2) & (row >= 1)),
    )
    mixes = (
        (0, (col == 3) & (row >= 1)),
        (1, (col >= 2) & (row >= 1)),
    )

    def send_terms(g):
        for part in range(2):
            xt[2 * g + part] = jnp.transpose(et[part]).astype(bf16)
        for level, ahead, cond in asides:
            @pl.when(cond)
            def _():
                term_aside(g, level, me + ahead).start()
        for level, cond in homes:
            @pl.when(cond & (me >= DISTANCES[level]))
            def _():
                term_home(g, level, me - DISTANCES[level]).start()

        def extra(i, _):
            @pl.when(me - gap_of(i) >= 0)
            def _():
                extra_term(g, i, me - gap_of(i)).start()
            return 0

        lax.fori_loop(0, len(FAR), extra, 0)

    def mix_terms(g):
        for level, cond in mixes:
            @pl.when(cond)
            def _():
                term_aside(g, level, me).wait_recv()
                tb[g, 2] = (tb[g, 2].astype(f32) + cr[g, level].astype(f32)).astype(bf16)

        @pl.when((col >= 2) & (row >= 1))
        def _():
            term_home(g, 2, me - 4).start()

    arrivals = (
        (0, (col <= 2) & (me + 1 < DEVICES)),
        (1, col <= 1),
        (2, me + 4 < DEVICES),
        (3, me + 8 < DEVICES),
    )

    def finish(g):
        for level, cond in arrivals:
            @pl.when(cond)
            def _():
                term_home(g, level, me).wait_recv()
                own[g] = own[g] + rb[g, level].astype(f32)

        def extra(i, _):
            @pl.when(me + gap_of(i) < DEVICES)
            def _():
                extra_term(g, i, me).wait_recv()
            return 0

        lax.fori_loop(0, len(FAR), extra, 0)
        for part, ref in enumerate((dk, dv)):
            folded = dot(spread[...], xr[2 * g + part], TN)
            ref[:, lanes(g)] = (jnp.transpose(own[g, part]) + folded).astype(bf16)

    lane = lax.broadcasted_iota(jnp.int32, (BLOCK, PAIR), 1)
    factor = math.log2(math.e) / math.sqrt(HD)
    scaling = 1.0 / math.sqrt(HD)

    def keys_of(g, c, part):
        if c == 0:
            return (k, v)[part][:, lanes(g)]
        if c < 5:
            return rx[g, c - 1, part]
        return xx[g, part]

    def features_of(head):
        return pl.ds(pl.multiple_of(head * HD, HD), HD)

    def only(head, array):
        return jnp.where((lane // HD) == head, array, jnp.zeros_like(array))

    def folded_lanes(array, op):
        result = array[:, :PAIR]
        for x in range(1, array.shape[1] // PAIR):
            result = op(result, array[:, x * PAIR:(x + 1) * PAIR])
        return result

    def attend(g, query, c):
        low, size = CHUNKS[c]
        scores = dot(query, keys_of(g, c, 0), NT) * factor
        if c == 0:
            r = lax.broadcasted_iota(jnp.int32, (BLOCK, BLOCK), 0)
            j = lax.broadcasted_iota(jnp.int32, (BLOCK, BLOCK), 1)
            scores = jnp.where(r >= j, scores, very_negative)
        else:
            scores = scores + bias[0:1, low:low + size]
        top = jnp.max(folded_lanes(scores, jnp.maximum), axis=1, keepdims=True)
        weights = jnp.exp2(scores - top)
        total = jnp.sum(folded_lanes(weights, jnp.add), axis=1, keepdims=True)
        weights = weights.astype(bf16)
        return top, weights, total, dot(weights, keys_of(g, c, 1), NN)

    def own_forward(i, _):
        g, head = i // 2, i % 2
        top, weights, total, mixed = attend(g, only(head, q[:, lanes(g)]), 0)
        p_own[i] = weights
        o_own[i] = mixed
        stats[i] = jnp.where(lane == 0, top, total)
        return 0

    def forward(g, head):
        i = 2 * g + head
        query = only(head, q[:, lanes(g)])
        tops, totals, mixes_ = [stats[i, :, 0:1]], [stats[i, :, 1:2]], [o_own[i]]
        for c in range(1, 6):
            low, size = CHUNKS[c]
            top, weights, total, mixed = attend(g, query, c)
            p_far[:, low - BLOCK:low - BLOCK + size] = weights
            tops.append(top)
            totals.append(total)
            mixes_.append(mixed)
        top = tops[0]
        for c in range(1, 6):
            top = jnp.maximum(top, tops[c])
        shares = [jnp.exp2(x - top) for x in tops]
        total = shares[0] * totals[0]
        for c in range(1, 6):
            total = total + shares[c] * totals[c]
        total = 1.0 / total
        shares = [share * total for share in shares]
        mixed = mixes_[0] * shares[0]
        for c in range(1, 6):
            mixed = mixed + mixes_[c] * shares[c]
        mixed = mixed.astype(bf16)
        grad = only(head, do[:, lanes(g)]).astype(f32)
        delta = jnp.sum(grad * mixed.astype(f32), axis=1, keepdims=True)
        o[:, lanes(g)] = jnp.where((lane // HD) == head, mixed, o[:, lanes(g)])
        columns = jnp.where(lane == 6, delta, 0.0)
        for c in range(6):
            columns = jnp.where(lane == c, shares[c], columns)
        stats[i] = columns
        share_rows[i] = jnp.transpose(columns)[0:8, :]

    def differentiate(g, head, c, grad, columns, weights):
        i = 2 * g + head
        share = columns[:, c:c + 1]
        keys = keys_of(g, c, 0)
        scaled = (grad * share).astype(bf16)
        scaled_t = (dt[g, features_of(head), :].astype(f32) * share_rows[i, c:c + 1, :]).astype(bf16)
        weight_grads = dot(scaled, keys_of(g, c, 1), NT)
        score_grads = (weights.astype(f32) * (weight_grads - columns[:, 6:7] * share)).astype(bf16)
        half = BLOCK // 2
        query_grad = jnp.concatenate(
            [dot(score_grads[:half], keys, NN), dot(score_grads[half:], keys, NN)], axis=0
        )
        key_term = dot(qt[g, features_of(head), :], score_grads, NN) * scaling
        return query_grad, key_term, dot(scaled_t, weights, NN)

    def backward(g, head):
        i = 2 * g + head
        grad = only(head, do[:, lanes(g)]).astype(f32)
        columns = stats[i]
        features = features_of(head)
        query_grad = jnp.zeros((BLOCK, PAIR), f32)
        for c in range(1, 6):
            low, size = CHUNKS[c]
            part_grad, *terms = differentiate(
                g, head, c, grad, columns, p_far[:, low - BLOCK:low - BLOCK + size]
            )
            query_grad = query_grad + part_grad
            for part, term in enumerate(terms):
                if c < 5:
                    tb[g, c - 1, part, features, :] = term.astype(bf16)
                else:
                    et[part, features, :] = term
        o_own[i] = query_grad

    def own_backward(i, _):
        g, head = i // 2, i % 2
        grad = only(head, do[:, lanes(g)]).astype(f32)
        part_grad, *terms = differentiate(g, head, 0, grad, stats[i], p_own[i])
        for part, term in enumerate(terms):
            own[g, part, features_of(head), :] = term
        query_grad = ((o_own[i] + part_grad) * scaling).astype(bf16)
        dq[:, lanes(g)] = jnp.where((lane // HD) == head, query_grad, dq[:, lanes(g)])
        return 0

    def transposed(a):
        return jnp.transpose(a.astype(f32)).astype(bf16)

    for g in range(GROUPS):
        qt[g] = transposed(q[:, g * PAIR:(g + 1) * PAIR])
        dt[g] = transposed(do[:, g * PAIR:(g + 1) * PAIR])
    o[...] = jnp.zeros_like(o)
    dq[...] = jnp.zeros_like(dq)

    def own_forwards(g, _):
        own_forward(2 * g, 0)
        own_forward(2 * g + 1, 0)
        return 0

    lax.fori_loop(0, GROUPS, own_forwards, 0)
    send_blocks(1)
    send_extras(1)

    def wait_extras(g):
        def one(i, _):
            @pl.when(me - gap_of(i) >= 0)
            def _():
                extra_copy(g, i, me).wait_recv()
            return 0

        lax.fori_loop(0, len(FAR), one, 0)

    def step(i, _):
        g = i // 2
        head = i % 2

        @pl.when(head == 0)
        def _():
            for level in (0, 1, 3):
                wait_blocks(g, level)
            wait_extras(g)

        @pl.when((head == 0) & (g + 2 < GROUPS))
        def _():
            send_blocks(g + 2)
            send_extras(g + 2)

        forward(g, head)

        @pl.when((head == 0) & (g + 1 < GROUPS))
        def _():
            relay_blocks(g + 1)

        backward(g, head)

        @pl.when((head == 1) & (g >= 1))
        def _():
            mix_terms(g - 1)

        @pl.when(head == 1)
        def _():
            send_terms(g)

        return 0

    lax.fori_loop(0, 2 * GROUPS, step, 0)

    def own_backwards(g, _):
        own_backward(2 * g, 0)
        own_backward(2 * g + 1, 0)
        return 0

    lax.fori_loop(0, GROUPS, own_backwards, 0)
    mix_terms(GROUPS - 1)

    def last(g, _):
        finish(g)
        return 0

    lax.fori_loop(0, GROUPS, last, 0)

    def left(g, _):
        for level, cond in direct:
            @pl.when(cond)
            def _():
                for copy in own_copies(g, level, me):
                    copy.wait_send()
        for level, back, cond in relays:
            @pl.when(cond)
            def _():
                for copy in relay_copies(g, level, me):
                    copy.wait_send()
        for level, distance in enumerate(DISTANCES):
            @pl.when(me >= distance)
            def _():
                term_home(g, level, me).wait_send()

        def extra(i, _):
            @pl.when(me + gap_of(i) < DEVICES)
            def _():
                extra_copy(g, i, me).wait_send()

            @pl.when(me - gap_of(i) >= 0)
            def _():
                extra_term(g, i, me).wait_send()
            return 0

        lax.fori_loop(0, len(FAR), extra, 0)
        return 0

    lax.fori_loop(0, GROUPS, left, 0)


def publish(*refs):
    for i in range(4):
        refs[i + 4][...] = refs[i][...]


def local(queries, key_rows, value_rows, grad_output, extra_blocks):
    whole = pl.BlockSpec(memory_space=pltpu.VMEM)
    slots = len(FAR)
    results = pl.pallas_call(
        kernel,
        out_shape=[jax.ShapeDtypeStruct((BLOCK, WIDTH), bf16)] * 4,
        in_specs=[whole] * 4 + [pl.BlockSpec(memory_space=pltpu.SMEM)],
        out_specs=[whole] * 4,
        scratch_shapes=[
            pltpu.VMEM((GROUPS, 4, 2, BLOCK, PAIR), bf16),
            pltpu.VMEM((GROUPS, 2, EXTRA_ROWS, PAIR), bf16),
            pltpu.VMEM((GROUPS, 2, EXTRA_ROWS, PAIR), bf16),
            pltpu.VMEM((GROUPS, 4, 2, PAIR, BLOCK), bf16),
            pltpu.VMEM((GROUPS, 2, PAIR, BLOCK), f32),
            pltpu.VMEM((2, PAIR, EXTRA_ROWS), f32),
            pltpu.VMEM((2 * GROUPS, EXTRA_ROWS, PAIR), bf16),
            pltpu.VMEM((GROUPS, 4, 2, PAIR, BLOCK), bf16),
            pltpu.VMEM((GROUPS, 2, 2, PAIR, BLOCK), bf16),
            pltpu.VMEM((2 * GROUPS, EXTRA_ROWS, PAIR), bf16),
            pltpu.VMEM((BLOCK, KEYS - BLOCK), bf16),
            pltpu.VMEM((2 * GROUPS, BLOCK, BLOCK), bf16),
            pltpu.VMEM((2 * GROUPS, BLOCK, PAIR), f32),
            pltpu.VMEM((2 * GROUPS, BLOCK, PAIR), f32),
            pltpu.VMEM((2 * GROUPS, 8, BLOCK), f32),
            pltpu.VMEM((GROUPS, PAIR, BLOCK), bf16),
            pltpu.VMEM((GROUPS, PAIR, BLOCK), bf16),
            pltpu.VMEM((8, KEYS), f32),
            pltpu.VMEM((EXTRA_ROWS, BLOCK), bf16),
            pltpu.SemaphoreType.DMA((GROUPS, 4, 2)),
            pltpu.SemaphoreType.DMA((GROUPS, 4, 2)),
            pltpu.SemaphoreType.DMA((GROUPS, 4, 2)),
            pltpu.SemaphoreType.DMA((GROUPS, slots)),
            pltpu.SemaphoreType.DMA((GROUPS, slots)),
            pltpu.SemaphoreType.DMA((GROUPS, 4)),
            pltpu.SemaphoreType.DMA((GROUPS, 4)),
            pltpu.SemaphoreType.DMA((GROUPS, 4)),
            pltpu.SemaphoreType.DMA((GROUPS, slots)),
            pltpu.SemaphoreType.DMA((GROUPS, slots)),
        ],
        compiler_params=pltpu.CompilerParams(
            collective_id=0, has_side_effects=True, vmem_limit_bytes=60 << 20
        ),
    )(queries, key_rows, value_rows, grad_output, extra_blocks)
    rows = pl.BlockSpec((BLOCK // 4, WIDTH), lambda i: (i, 0))
    return pl.pallas_call(
        publish,
        grid=(4,),
        out_shape=[jax.ShapeDtypeStruct((BLOCK, WIDTH), bf16)] * 4,
        in_specs=[rows] * 4,
        out_specs=[rows] * 4,
    )(*results)


def solution(mesh):
    rows = P(("member", "tm"), None)
    return jax.shard_map(
        local,
        mesh=mesh,
        in_specs=(rows, rows, rows, rows, P("member", None)),
        out_specs=(rows, rows, rows, rows),
        check_vma=False,
    )
```

```python
import math

import jax
import jax.numpy as jnp
from jax import lax
from jax.experimental import pallas as pl
from jax.experimental.pallas import tpu as pltpu
from jax.sharding import PartitionSpec as P

HD = 64
SUB = 16
CAP = 2
MESH = pl.DeviceIdType.MESH
NT = (((1,), (1,)), ((), ()))
NN = (((1,), (0,)), ((), ()))
TN = (((0,), (0,)), ((), ()))
very_negative = -1e30
f32 = jnp.float32
bf16 = jnp.bfloat16

DEVICES = 16
SIDE = 4
BLOCK = 512
WIDTH = 512
PAIR = 128
GROUPS = WIDTH // PAIR
PER_BLOCK = BLOCK // SUB
DISTANCES = (1, 2, 4, 8)
FAR = tuple(d for d in range(1, DEVICES) if d not in DISTANCES)
SLOT_ROWS = CAP * SUB
LAG = 2
EXTRA_ROWS = 384
KEYS = 5 * BLOCK + EXTRA_ROWS
CHUNKS = tuple((i * BLOCK, BLOCK) for i in range(5)) + ((5 * BLOCK, EXTRA_ROWS),)


def dot(a, b, dims):
    return lax.dot_general(a, b, dims, preferred_element_type=f32)


def kernel(
    q, k, v, do, table,
    o, dq, dk, dv,
    rx, xx, xs, tb, own, et, xt, rb, cr, xr,
    p_far, p_own, o_own, stats, share_rows, qt, dt, bias, spread,
    send_kv, recv_kv, send_relay, send_x, recv_x,
    send_t, recv_t, recv_c, send_xt, recv_xt,
):
    me = lax.axis_index("tm")
    col = lax.rem(me, SIDE)
    row = me // SIDE

    def device(index):
        return {"tm": index}

    barrier = pltpu.get_barrier_semaphore()
    for i in range(DEVICES):
        @pl.when(me != i)
        def _():
            pl.semaphore_signal(barrier, inc=1, device_id=device(i), device_id_type=MESH)
    pl.semaphore_wait(barrier, DEVICES - 1)

    def lanes(g):
        return pl.ds(pl.multiple_of(g * PAIR, PAIR), PAIR)

    def kv_copies(g, level, src_k, src_v, send, to):
        return [
            pltpu.make_async_remote_copy(
                src_ref=src,
                dst_ref=rx.at[g, level, part],
                send_sem=send.at[g, level, part],
                recv_sem=recv_kv.at[g, level, part],
                device_id=device(to),
                device_id_type=MESH,
            )
            for part, src in enumerate((src_k, src_v))
        ]

    def own_copies(g, level, to):
        return kv_copies(g, level, k.at[:, lanes(g)], v.at[:, lanes(g)], send_kv, to)

    def relay_copies(g, level, to):
        return kv_copies(g, level, rx.at[g, 2, 0], rx.at[g, 2, 1], send_relay, to)

    direct = (
        (2, me + 4 < DEVICES),
        (0, (col < 3) & (me + 1 < DEVICES)),
        (1, col < 2),
    )
    farthest = (3, me + 8 < DEVICES)
    relays = (
        (0, 3, (col == 3) & (row >= 1)),
        (1, 2, (col >= 2) & (row >= 1)),
    )

    def send_part(g, part, targets):
        for level, cond in targets:
            @pl.when(cond)
            def _():
                own_copies(g, level, me + DISTANCES[level])[part].start()

    def send_blocks(g):
        for part in range(2):
            send_part(g, part, direct)

    def wait_part(g, level, part):
        @pl.when(me >= DISTANCES[level])
        def _():
            own_copies(g, level, me)[part].wait_recv()

    def wait_blocks(g, level):
        for part in range(2):
            wait_part(g, level, part)

    def relay_part(g, part):
        wait_part(g, 2, part)
        for level, back, cond in relays:
            @pl.when(cond)
            def _():
                relay_copies(g, level, me - back)[part].start()

    def relay_blocks(g):
        for part in range(2):
            relay_part(g, part)
        for part in range(2):
            send_part(g, part, (farthest,))

    send_part(0, 0, direct)

    def gap_of(i):
        return i + 3 + (i + 10) // 11 + (i + 7) // 11

    def extra_copy(g, i, to):
        rows = pl.ds(pl.multiple_of(i * SLOT_ROWS, SLOT_ROWS), SLOT_ROWS)
        return pltpu.make_async_remote_copy(
            src_ref=xs.at[g, :, rows, :],
            dst_ref=xx.at[g, :, rows, :],
            send_sem=send_x.at[g, i],
            recv_sem=recv_x.at[g, i],
            device_id=device(to),
            device_id_type=MESH,
        )

    spread[...] = jnp.zeros_like(spread)

    def find(i, _):
        other = me + gap_of(i)

        @pl.when(other < DEVICES)
        def _():
            first = me * PER_BLOCK
            count = jnp.int32(0)
            index = [jnp.int32(0), jnp.int32(0)]
            for n in range(table.shape[1]):
                entry = table[other, n]
                inside = entry - first
                mine = (inside >= 0) & (inside < PER_BLOCK)
                for slot in range(CAP):
                    index[slot] = jnp.where(mine & (count == slot), inside, index[slot])
                count = count + jnp.where(mine, 1, 0)
            for slot in range(CAP):
                base = jnp.where(count > slot, index[slot] * SUB, jnp.int32(-4096))
                hit = lax.broadcasted_iota(jnp.int32, (SUB, BLOCK), 1) == (
                    lax.broadcasted_iota(jnp.int32, (SUB, BLOCK), 0) + base
                )
                spread[pl.ds(pl.multiple_of(i * SLOT_ROWS + slot * SUB, SUB), SUB), :] = jnp.where(
                    hit, 1.0, 0.0
                ).astype(bf16)

        return 0

    lax.fori_loop(0, len(FAR), find, 0)
    for part, ref in enumerate((k, v)):
        for g in range(GROUPS):
            xs[g, part] = dot(spread[...], ref[:, g * PAIR:(g + 1) * PAIR], NN).astype(bf16)

    def send_extras(g):
        def one(i, _):
            @pl.when(me + gap_of(i) < DEVICES)
            def _():
                extra_copy(g, i, me + gap_of(i)).start()
            return 0

        lax.fori_loop(0, len(FAR), one, 0)

    relay_part(0, 0)
    send_part(0, 1, direct)

    key_row = lax.broadcasted_iota(jnp.int32, (8, BLOCK), 1)
    for level, distance in enumerate(DISTANCES):
        sub_block = (me - distance) * PER_BLOCK + (key_row >> 4)
        times = jnp.zeros((8, BLOCK), f32)
        for n in range(table.shape[1]):
            times = times + jnp.where(sub_block == table[me, n], 1.0, 0.0)
        value = jnp.where(times > 0.5, 1.0, 0.0)
        low, size = CHUNKS[1 + level]
        bias[:, low:low + size] = jnp.where(sub_block >= 0, value, very_negative)
    key_row = lax.broadcasted_iota(jnp.int32, (8, EXTRA_ROWS), 1)
    place = key_row >> 5
    owner = me - (place + 3 + jnp.where(place >= 1, 1, 0) + jnp.where(place >= 4, 1, 0))
    times = jnp.zeros((8, EXTRA_ROWS), f32)
    for n in range(table.shape[1]):
        entry = table[me, n]
        inside = entry - owner * PER_BLOCK
        times = times + jnp.where((inside >= 0) & (inside < PER_BLOCK), 1.0, 0.0)
    slot_of = ((key_row >> 4) & 1).astype(f32)
    live = (times > slot_of + 0.5) & (owner >= 0) & (place < len(FAR))
    bias[:, 5 * BLOCK:] = jnp.where(live, 0.0, very_negative)

    for level, distance in enumerate(DISTANCES):
        @pl.when(me < distance)
        def _():
            def clear(g, _):
                rx[g, level] = jnp.zeros(rx.shape[2:], bf16)
                return 0
            lax.fori_loop(0, GROUPS, clear, 0)
    tail = len(FAR) * SLOT_ROWS
    xx[:, :, tail:, :] = jnp.zeros((GROUPS, 2, EXTRA_ROWS - tail, PAIR), bf16)
    xr[:, tail:, :] = jnp.zeros((2 * GROUPS, EXTRA_ROWS - tail, PAIR), bf16)

    def clear_extra(i, _):
        rows = pl.ds(pl.multiple_of(i * SLOT_ROWS, SLOT_ROWS), SLOT_ROWS)

        @pl.when(me - gap_of(i) < 0)
        def _():
            xx[:, :, rows, :] = jnp.zeros((GROUPS, 2, SLOT_ROWS, PAIR), bf16)

        @pl.when(me + gap_of(i) >= DEVICES)
        def _():
            xr[:, rows, :] = jnp.zeros((2 * GROUPS, SLOT_ROWS, PAIR), bf16)

        return 0

    lax.fori_loop(0, len(FAR), clear_extra, 0)

    def term_rows(i):
        return i // 2, pl.ds(pl.multiple_of((i % 2) * HD, HD), HD)

    def term_copy(i, level, place, recv, to):
        g, rows = term_rows(i)
        return pltpu.make_async_remote_copy(
            src_ref=tb.at[g, level, :, rows, :],
            dst_ref=place.at[g, level, :, rows, :],
            send_sem=send_t.at[i, level],
            recv_sem=recv.at[i, level],
            device_id=device(to),
            device_id_type=MESH,
        )

    def term_home(i, level, to):
        return term_copy(i, level, rb, recv_t, to)

    def term_aside(i, level, to):
        return term_copy(i, level, cr, recv_c, to)

    def extra_term(g, i, to):
        rows = pl.ds(pl.multiple_of(i * SLOT_ROWS, SLOT_ROWS), SLOT_ROWS)
        both = pl.ds(2 * g, 2)
        return pltpu.make_async_remote_copy(
            src_ref=xt.at[both, rows, :],
            dst_ref=xr.at[both, rows, :],
            send_sem=send_xt.at[g, i],
            recv_sem=recv_xt.at[g, i],
            device_id=device(to),
            device_id_type=MESH,
        )

    homes = (
        (0, col >= 1),
        (1, col >= 2),
        (3, me >= 8),
        (2, (col < 2) & (row >= 1)),
    )
    asides = (
        (0, 3, (col == 0) & (row >= 1)),
        (1, 2, (col < 2) & (row >= 1)),
    )
    mixes = (
        (0, (col == 3) & (row >= 1)),
        (1, (col >= 2) & (row >= 1)),
    )

    def send_terms(i):
        for level, ahead, cond in asides:
            @pl.when(cond)
            def _():
                term_aside(i, level, me + ahead).start()
        for level, cond in homes:
            @pl.when(cond & (me >= DISTANCES[level]))
            def _():
                term_home(i, level, me - DISTANCES[level]).start()

    def send_extra_terms(g):
        for part in range(2):
            xt[2 * g + part] = jnp.transpose(et[part]).astype(bf16)

        def extra(i, _):
            @pl.when(me - gap_of(i) >= 0)
            def _():
                extra_term(g, i, me - gap_of(i)).start()
            return 0

        lax.fori_loop(0, len(FAR), extra, 0)

    def mix_terms(i):
        g, rows = term_rows(i)
        for level, cond in mixes:
            @pl.when(cond)
            def _():
                term_aside(i, level, me).wait_recv()
                tb[g, 2, :, rows, :] = (
                    tb[g, 2, :, rows, :].astype(f32) + cr[g, level, :, rows, :].astype(f32)
                ).astype(bf16)

        @pl.when((col >= 2) & (row >= 1))
        def _():
            term_home(i, 2, me - 4).start()

    arrivals = (
        (0, (col <= 2) & (me + 1 < DEVICES)),
        (1, col <= 1),
        (2, me + 4 < DEVICES),
        (3, me + 8 < DEVICES),
    )

    def finish(g):
        for level, cond in arrivals:
            @pl.when(cond)
            def _():
                term_home(2 * g, level, me).wait_recv()
                term_home(2 * g + 1, level, me).wait_recv()
                own[g] = own[g] + rb[g, level].astype(f32)

        def extra(i, _):
            @pl.when(me + gap_of(i) < DEVICES)
            def _():
                extra_term(g, i, me).wait_recv()
            return 0

        lax.fori_loop(0, len(FAR), extra, 0)
        for part, ref in enumerate((dk, dv)):
            folded = dot(spread[...], xr[2 * g + part], TN)
            ref[:, lanes(g)] = (jnp.transpose(own[g, part]) + folded).astype(bf16)

    lane = lax.broadcasted_iota(jnp.int32, (BLOCK, PAIR), 1)
    factor = math.log2(math.e) / math.sqrt(HD)
    scaling = 1.0 / math.sqrt(HD)

    def keys_of(g, c, part):
        if c == 0:
            return (k, v)[part][:, lanes(g)]
        if c < 5:
            return rx[g, c - 1, part]
        return xx[g, part]

    def features_of(head):
        return pl.ds(pl.multiple_of(head * HD, HD), HD)

    def only(head, array):
        return jnp.where((lane // HD) == head, array, jnp.zeros_like(array))

    def folded_lanes(array, op):
        result = array[:, :PAIR]
        for x in range(1, array.shape[1] // PAIR):
            result = op(result, array[:, x * PAIR:(x + 1) * PAIR])
        return result

    def attend(g, query, c):
        low, size = CHUNKS[c]
        scores = dot(query, keys_of(g, c, 0), NT) * factor
        if c == 0:
            r = lax.broadcasted_iota(jnp.int32, (BLOCK, BLOCK), 0)
            j = lax.broadcasted_iota(jnp.int32, (BLOCK, BLOCK), 1)
            scores = jnp.where(r >= j, scores, very_negative)
        else:
            scores = scores + bias[0:1, low:low + size]
        top = jnp.max(folded_lanes(scores, jnp.maximum), axis=1, keepdims=True)
        weights = jnp.exp2(scores - top)
        total = jnp.sum(folded_lanes(weights, jnp.add), axis=1, keepdims=True)
        weights = weights.astype(bf16)
        return top, weights, total, dot(weights, keys_of(g, c, 1), NN)

    def own_forward(i, _):
        g, head = i // 2, i % 2
        top, weights, total, mixed = attend(g, only(head, q[:, lanes(g)]), 0)
        p_own[i] = weights
        o_own[i] = mixed
        stats[i] = jnp.where(lane == 0, top, total)
        return 0

    def forward(g, head):
        i = 2 * g + head
        query = only(head, q[:, lanes(g)])
        tops, totals, mixes_ = [stats[i, :, 0:1]], [stats[i, :, 1:2]], [o_own[i]]
        for c in range(1, 6):
            low, size = CHUNKS[c]
            top, weights, total, mixed = attend(g, query, c)
            p_far[:, low - BLOCK:low - BLOCK + size] = weights
            tops.append(top)
            totals.append(total)
            mixes_.append(mixed)
        top = tops[0]
        for c in range(1, 6):
            top = jnp.maximum(top, tops[c])
        shares = [jnp.exp2(x - top) for x in tops]
        total = shares[0] * totals[0]
        for c in range(1, 6):
            total = total + shares[c] * totals[c]
        total = 1.0 / total
        shares = [share * total for share in shares]
        mixed = mixes_[0] * shares[0]
        for c in range(1, 6):
            mixed = mixed + mixes_[c] * shares[c]
        mixed = mixed.astype(bf16)
        grad = only(head, do[:, lanes(g)]).astype(f32)
        delta = jnp.sum(grad * mixed.astype(f32), axis=1, keepdims=True)
        o[:, lanes(g)] = jnp.where((lane // HD) == head, mixed, o[:, lanes(g)])
        columns = jnp.where(lane == 6, delta, 0.0)
        for c in range(6):
            columns = jnp.where(lane == c, shares[c], columns)
        stats[i] = columns
        share_rows[i] = jnp.transpose(columns)[0:8, :]

    def differentiate(g, head, c, grad, columns, weights):
        i = 2 * g + head
        share = columns[:, c:c + 1]
        keys = keys_of(g, c, 0)
        scaled = (grad * share).astype(bf16)
        scaled_t = (dt[g, features_of(head), :].astype(f32) * share_rows[i, c:c + 1, :]).astype(bf16)
        weight_grads = dot(scaled, keys_of(g, c, 1), NT)
        score_grads = (weights.astype(f32) * (weight_grads - columns[:, 6:7] * share)).astype(bf16)
        half = BLOCK // 2
        query_grad = jnp.concatenate(
            [dot(score_grads[:half], keys, NN), dot(score_grads[half:], keys, NN)], axis=0
        )
        key_term = dot(qt[g, features_of(head), :], score_grads, NN) * scaling
        return query_grad, key_term, dot(scaled_t, weights, NN)

    def backward(g, head):
        i = 2 * g + head
        grad = only(head, do[:, lanes(g)]).astype(f32)
        columns = stats[i]
        features = features_of(head)
        query_grad = jnp.zeros((BLOCK, PAIR), f32)
        for c in range(1, 6):
            low, size = CHUNKS[c]
            part_grad, *terms = differentiate(
                g, head, c, grad, columns, p_far[:, low - BLOCK:low - BLOCK + size]
            )
            query_grad = query_grad + part_grad
            for part, term in enumerate(terms):
                if c < 5:
                    tb[g, c - 1, part, features, :] = term.astype(bf16)
                else:
                    et[part, features, :] = term
        o_own[i] = query_grad

    def own_backward(i, _):
        g, head = i // 2, i % 2
        grad = only(head, do[:, lanes(g)]).astype(f32)
        part_grad, *terms = differentiate(g, head, 0, grad, stats[i], p_own[i])
        for part, term in enumerate(terms):
            own[g, part, features_of(head), :] = term
        query_grad = ((o_own[i] + part_grad) * scaling).astype(bf16)
        dq[:, lanes(g)] = jnp.where((lane // HD) == head, query_grad, dq[:, lanes(g)])
        return 0

    def transposed(a):
        return jnp.transpose(a.astype(f32)).astype(bf16)

    for g in range(GROUPS):
        qt[g] = transposed(q[:, g * PAIR:(g + 1) * PAIR])
        dt[g] = transposed(do[:, g * PAIR:(g + 1) * PAIR])
    o[...] = jnp.zeros_like(o)
    dq[...] = jnp.zeros_like(dq)

    def own_forwards(g, _):
        own_forward(2 * g, 0)
        own_forward(2 * g + 1, 0)
        return 0

    lax.fori_loop(0, GROUPS // 2, own_forwards, 0)
    relay_part(0, 1)
    for part in range(2):
        send_part(0, part, (farthest,))
    send_extras(0)
    lax.fori_loop(GROUPS // 2, GROUPS, own_forwards, 0)

    def wait_extras(g):
        def one(i, _):
            @pl.when(me - gap_of(i) >= 0)
            def _():
                extra_copy(g, i, me).wait_recv()
            return 0

        lax.fori_loop(0, len(FAR), one, 0)

    def step(i, _):
        g = i // 2
        head = i % 2

        @pl.when(head == 0)
        def _():
            for level in (0, 1, 3):
                wait_blocks(g, level)
            wait_extras(g)

        @pl.when((head == 0) & (g + 1 < GROUPS))
        def _():
            send_blocks(g + 1)

        forward(g, head)

        @pl.when((head == 1) & (g + 1 < GROUPS))
        def _():
            relay_blocks(g + 1)
            send_extras(g + 1)

        backward(g, head)

        @pl.when(i >= LAG)
        def _():
            mix_terms(i - LAG)

        send_terms(i)

        @pl.when(head == 1)
        def _():
            send_extra_terms(g)

        return 0

    lax.fori_loop(0, 2 * GROUPS, step, 0)

    def own_backwards(g, _):
        own_backward(2 * g, 0)
        own_backward(2 * g + 1, 0)
        return 0

    lax.fori_loop(0, GROUPS // 2, own_backwards, 0)

    def late_mix(i, _):
        mix_terms(i)
        return 0

    lax.fori_loop(2 * GROUPS - LAG, 2 * GROUPS, late_mix, 0)
    lax.fori_loop(GROUPS // 2, GROUPS, own_backwards, 0)

    def last(g, _):
        finish(g)
        return 0

    lax.fori_loop(0, GROUPS, last, 0)

    def left(g, _):
        for level, cond in direct + (farthest,):
            @pl.when(cond)
            def _():
                for copy in own_copies(g, level, me):
                    copy.wait_send()
        for level, back, cond in relays:
            @pl.when(cond)
            def _():
                for copy in relay_copies(g, level, me):
                    copy.wait_send()
        for level, distance in enumerate(DISTANCES):
            @pl.when(me >= distance)
            def _():
                term_home(2 * g, level, me).wait_send()
                term_home(2 * g + 1, level, me).wait_send()

        def extra(i, _):
            @pl.when(me + gap_of(i) < DEVICES)
            def _():
                extra_copy(g, i, me).wait_send()

            @pl.when(me - gap_of(i) >= 0)
            def _():
                extra_term(g, i, me).wait_send()
            return 0

        lax.fori_loop(0, len(FAR), extra, 0)
        return 0

    lax.fori_loop(0, GROUPS, left, 0)


def publish(*refs):
    for i in range(4):
        refs[i + 4][...] = refs[i][...]


def local(queries, key_rows, value_rows, grad_output, extra_blocks):
    whole = pl.BlockSpec(memory_space=pltpu.VMEM)
    slots = len(FAR)
    results = pl.pallas_call(
        kernel,
        out_shape=[jax.ShapeDtypeStruct((BLOCK, WIDTH), bf16)] * 4,
        in_specs=[whole] * 4 + [pl.BlockSpec(memory_space=pltpu.SMEM)],
        out_specs=[whole] * 4,
        scratch_shapes=[
            pltpu.VMEM((GROUPS, 4, 2, BLOCK, PAIR), bf16),
            pltpu.VMEM((GROUPS, 2, EXTRA_ROWS, PAIR), bf16),
            pltpu.VMEM((GROUPS, 2, EXTRA_ROWS, PAIR), bf16),
            pltpu.VMEM((GROUPS, 4, 2, PAIR, BLOCK), bf16),
            pltpu.VMEM((GROUPS, 2, PAIR, BLOCK), f32),
            pltpu.VMEM((2, PAIR, EXTRA_ROWS), f32),
            pltpu.VMEM((2 * GROUPS, EXTRA_ROWS, PAIR), bf16),
            pltpu.VMEM((GROUPS, 4, 2, PAIR, BLOCK), bf16),
            pltpu.VMEM((GROUPS, 2, 2, PAIR, BLOCK), bf16),
            pltpu.VMEM((2 * GROUPS, EXTRA_ROWS, PAIR), bf16),
            pltpu.VMEM((BLOCK, KEYS - BLOCK), bf16),
            pltpu.VMEM((2 * GROUPS, BLOCK, BLOCK), bf16),
            pltpu.VMEM((2 * GROUPS, BLOCK, PAIR), f32),
            pltpu.VMEM((2 * GROUPS, BLOCK, PAIR), f32),
            pltpu.VMEM((2 * GROUPS, 8, BLOCK), f32),
            pltpu.VMEM((GROUPS, PAIR, BLOCK), bf16),
            pltpu.VMEM((GROUPS, PAIR, BLOCK), bf16),
            pltpu.VMEM((8, KEYS), f32),
            pltpu.VMEM((EXTRA_ROWS, BLOCK), bf16),
            pltpu.SemaphoreType.DMA((GROUPS, 4, 2)),
            pltpu.SemaphoreType.DMA((GROUPS, 4, 2)),
            pltpu.SemaphoreType.DMA((GROUPS, 4, 2)),
            pltpu.SemaphoreType.DMA((GROUPS, slots)),
            pltpu.SemaphoreType.DMA((GROUPS, slots)),
            pltpu.SemaphoreType.DMA((2 * GROUPS, 4)),
            pltpu.SemaphoreType.DMA((2 * GROUPS, 4)),
            pltpu.SemaphoreType.DMA((2 * GROUPS, 4)),
            pltpu.SemaphoreType.DMA((GROUPS, slots)),
            pltpu.SemaphoreType.DMA((GROUPS, slots)),
        ],
        compiler_params=pltpu.CompilerParams(
            collective_id=0, has_side_effects=True, vmem_limit_bytes=60 << 20
        ),
    )(queries, key_rows, value_rows, grad_output, extra_blocks)
    return pl.pallas_call(
        publish,
        out_shape=[jax.ShapeDtypeStruct((BLOCK, WIDTH), bf16)] * 4,
        in_specs=[whole] * 4,
        out_specs=[whole] * 4,
    )(*results)


def solution(mesh):
    rows = P(("member", "tm"), None)
    return jax.shard_map(
        local,
        mesh=mesh,
        in_specs=(rows, rows, rows, rows, P("member", None)),
        out_specs=(rows, rows, rows, rows),
        check_vma=False,
    )
```

```python
import math

import jax
import jax.numpy as jnp
from jax import lax
from jax.experimental import pallas as pl
from jax.experimental.pallas import tpu as pltpu
from jax.sharding import PartitionSpec as P

HD = 64
SUB = 16
CAP = 2
MESH = pl.DeviceIdType.MESH
NT = (((1,), (1,)), ((), ()))
NN = (((1,), (0,)), ((), ()))
TN = (((0,), (0,)), ((), ()))
very_negative = -1e30
f32 = jnp.float32
bf16 = jnp.bfloat16

DEVICES = 16
SIDE = 4
BLOCK = 512
WIDTH = 512
PAIR = 128
GROUPS = WIDTH // PAIR
PER_BLOCK = BLOCK // SUB
DISTANCES = (1, 2, 4, 8)
FAR = tuple(d for d in range(1, DEVICES) if d not in DISTANCES)
SLOT_ROWS = CAP * SUB
LAG = 2
EXTRA_ROWS = 384
KEYS = 5 * BLOCK + EXTRA_ROWS
CHUNKS = tuple((i * BLOCK, BLOCK) for i in range(5)) + ((5 * BLOCK, EXTRA_ROWS),)


def dot(a, b, dims):
    return lax.dot_general(a, b, dims, preferred_element_type=f32)


def kernel(
    q, k, v, do, table,
    o, dq, dk, dv,
    rx, xx, xs, tb, own, et, xt, rb, cr, xr,
    p_far, p_own, o_own, stats, share_rows, qt, dt, bias, spread,
    send_kv, recv_kv, send_relay, send_x, recv_x,
    send_t, recv_t, recv_c, send_xt, recv_xt,
):
    me = lax.axis_index("tm")
    col = lax.rem(me, SIDE)
    row = me // SIDE

    def device(index):
        return {"tm": index}

    barrier = pltpu.get_barrier_semaphore()
    for i in range(DEVICES):
        @pl.when(me != i)
        def _():
            pl.semaphore_signal(barrier, inc=1, device_id=device(i), device_id_type=MESH)
    pl.semaphore_wait(barrier, DEVICES - 1)

    def lanes(g):
        return pl.ds(pl.multiple_of(g * PAIR, PAIR), PAIR)

    def kv_copies(g, level, src_k, src_v, send, to):
        return [
            pltpu.make_async_remote_copy(
                src_ref=src,
                dst_ref=rx.at[g, level, part],
                send_sem=send.at[g, level, part],
                recv_sem=recv_kv.at[g, level, part],
                device_id=device(to),
                device_id_type=MESH,
            )
            for part, src in enumerate((src_k, src_v))
        ]

    def own_copies(g, level, to):
        return kv_copies(g, level, k.at[:, lanes(g)], v.at[:, lanes(g)], send_kv, to)

    def relay_copies(g, level, to):
        return kv_copies(g, level, rx.at[g, 2, 0], rx.at[g, 2, 1], send_relay, to)

    relayed = ((2, me + 4 < DEVICES),)
    nearest = (
        (0, (col < 3) & (me + 1 < DEVICES)),
        (1, col < 2),
    )
    direct = relayed + nearest
    farthest = (3, me + 8 < DEVICES)
    relays = (
        (0, 3, (col == 3) & (row >= 1)),
        (1, 2, (col >= 2) & (row >= 1)),
    )

    def send_part(g, part, targets):
        for level, cond in targets:
            @pl.when(cond)
            def _():
                own_copies(g, level, me + DISTANCES[level])[part].start()

    def send_both(g, targets):
        for part in range(2):
            send_part(g, part, targets)

    def wait_part(g, level, part):
        @pl.when(me >= DISTANCES[level])
        def _():
            own_copies(g, level, me)[part].wait_recv()

    def wait_blocks(g, level):
        for part in range(2):
            wait_part(g, level, part)

    def relay_part(g, part):
        wait_part(g, 2, part)
        for level, back, cond in relays:
            @pl.when(cond)
            def _():
                relay_copies(g, level, me - back)[part].start()

    def relay_blocks(g):
        for part in range(2):
            relay_part(g, part)

    send_part(0, 0, direct)

    def gap_of(i):
        return i + 3 + (i + 10) // 11 + (i + 7) // 11

    def extra_copy(g, i, to):
        rows = pl.ds(pl.multiple_of(i * SLOT_ROWS, SLOT_ROWS), SLOT_ROWS)
        return pltpu.make_async_remote_copy(
            src_ref=xs.at[g, :, rows, :],
            dst_ref=xx.at[g, :, rows, :],
            send_sem=send_x.at[g, i],
            recv_sem=recv_x.at[g, i],
            device_id=device(to),
            device_id_type=MESH,
        )

    spread[...] = jnp.zeros_like(spread)

    def find(i, _):
        other = me + gap_of(i)

        @pl.when(other < DEVICES)
        def _():
            first = me * PER_BLOCK
            count = jnp.int32(0)
            index = [jnp.int32(0), jnp.int32(0)]
            for n in range(table.shape[1]):
                entry = table[other, n]
                inside = entry - first
                mine = (inside >= 0) & (inside < PER_BLOCK)
                for slot in range(CAP):
                    index[slot] = jnp.where(mine & (count == slot), inside, index[slot])
                count = count + jnp.where(mine, 1, 0)
            for slot in range(CAP):
                base = jnp.where(count > slot, index[slot] * SUB, jnp.int32(-4096))
                hit = lax.broadcasted_iota(jnp.int32, (SUB, BLOCK), 1) == (
                    lax.broadcasted_iota(jnp.int32, (SUB, BLOCK), 0) + base
                )
                spread[pl.ds(pl.multiple_of(i * SLOT_ROWS + slot * SUB, SUB), SUB), :] = jnp.where(
                    hit, 1.0, 0.0
                ).astype(bf16)

        return 0

    lax.fori_loop(0, len(FAR), find, 0)
    for part, ref in enumerate((k, v)):
        for g in range(GROUPS):
            xs[g, part] = dot(spread[...], ref[:, g * PAIR:(g + 1) * PAIR], NN).astype(bf16)

    def send_extras(g):
        def one(i, _):
            @pl.when(me + gap_of(i) < DEVICES)
            def _():
                extra_copy(g, i, me + gap_of(i)).start()
            return 0

        lax.fori_loop(0, len(FAR), one, 0)

    relay_part(0, 0)
    send_part(0, 1, direct)

    key_row = lax.broadcasted_iota(jnp.int32, (8, BLOCK), 1)
    for level, distance in enumerate(DISTANCES):
        sub_block = (me - distance) * PER_BLOCK + (key_row >> 4)
        times = jnp.zeros((8, BLOCK), f32)
        for n in range(table.shape[1]):
            times = times + jnp.where(sub_block == table[me, n], 1.0, 0.0)
        value = jnp.where(times > 0.5, 1.0, 0.0)
        low, size = CHUNKS[1 + level]
        bias[:, low:low + size] = jnp.where(sub_block >= 0, value, very_negative)
    key_row = lax.broadcasted_iota(jnp.int32, (8, EXTRA_ROWS), 1)
    place = key_row >> 5
    owner = me - (place + 3 + jnp.where(place >= 1, 1, 0) + jnp.where(place >= 4, 1, 0))
    times = jnp.zeros((8, EXTRA_ROWS), f32)
    for n in range(table.shape[1]):
        entry = table[me, n]
        inside = entry - owner * PER_BLOCK
        times = times + jnp.where((inside >= 0) & (inside < PER_BLOCK), 1.0, 0.0)
    slot_of = ((key_row >> 4) & 1).astype(f32)
    live = (times > slot_of + 0.5) & (owner >= 0) & (place < len(FAR))
    bias[:, 5 * BLOCK:] = jnp.where(live, 0.0, very_negative)

    for level, distance in enumerate(DISTANCES):
        @pl.when(me < distance)
        def _():
            def clear(g, _):
                rx[g, level] = jnp.zeros(rx.shape[2:], bf16)
                return 0
            lax.fori_loop(0, GROUPS, clear, 0)
    tail = len(FAR) * SLOT_ROWS
    xx[:, :, tail:, :] = jnp.zeros((GROUPS, 2, EXTRA_ROWS - tail, PAIR), bf16)
    xr[:, tail:, :] = jnp.zeros((2 * GROUPS, EXTRA_ROWS - tail, PAIR), bf16)

    def clear_extra(i, _):
        rows = pl.ds(pl.multiple_of(i * SLOT_ROWS, SLOT_ROWS), SLOT_ROWS)

        @pl.when(me - gap_of(i) < 0)
        def _():
            xx[:, :, rows, :] = jnp.zeros((GROUPS, 2, SLOT_ROWS, PAIR), bf16)

        @pl.when(me + gap_of(i) >= DEVICES)
        def _():
            xr[:, rows, :] = jnp.zeros((2 * GROUPS, SLOT_ROWS, PAIR), bf16)

        return 0

    lax.fori_loop(0, len(FAR), clear_extra, 0)

    def term_rows(i):
        return i // 2, pl.ds(pl.multiple_of((i % 2) * HD, HD), HD)

    def term_copy(i, level, place, recv, to):
        g, rows = term_rows(i)
        return pltpu.make_async_remote_copy(
            src_ref=tb.at[g, level, :, rows, :],
            dst_ref=place.at[g, level, :, rows, :],
            send_sem=send_t.at[i, level],
            recv_sem=recv.at[i, level],
            device_id=device(to),
            device_id_type=MESH,
        )

    def term_home(i, level, to):
        return term_copy(i, level, rb, recv_t, to)

    def term_aside(i, level, to):
        return term_copy(i, level, cr, recv_c, to)

    def extra_term(g, i, to):
        rows = pl.ds(pl.multiple_of(i * SLOT_ROWS, SLOT_ROWS), SLOT_ROWS)
        both = pl.ds(2 * g, 2)
        return pltpu.make_async_remote_copy(
            src_ref=xt.at[both, rows, :],
            dst_ref=xr.at[both, rows, :],
            send_sem=send_xt.at[g, i],
            recv_sem=recv_xt.at[g, i],
            device_id=device(to),
            device_id_type=MESH,
        )

    homes = (
        (0, col >= 1),
        (1, col >= 2),
        (3, me >= 8),
        (2, (col < 2) & (row >= 1)),
    )
    asides = (
        (0, 3, (col == 0) & (row >= 1)),
        (1, 2, (col < 2) & (row >= 1)),
    )
    mixes = (
        (0, (col == 3) & (row >= 1)),
        (1, (col >= 2) & (row >= 1)),
    )

    def send_terms(i):
        for level, ahead, cond in asides:
            @pl.when(cond)
            def _():
                term_aside(i, level, me + ahead).start()
        for level, cond in homes:
            @pl.when(cond & (me >= DISTANCES[level]))
            def _():
                term_home(i, level, me - DISTANCES[level]).start()

    def send_extra_terms(g):
        for part in range(2):
            xt[2 * g + part] = jnp.transpose(et[part]).astype(bf16)

        def extra(i, _):
            @pl.when(me - gap_of(i) >= 0)
            def _():
                extra_term(g, i, me - gap_of(i)).start()
            return 0

        lax.fori_loop(0, len(FAR), extra, 0)

    def mix_terms(i):
        g, rows = term_rows(i)
        for level, cond in mixes:
            @pl.when(cond)
            def _():
                term_aside(i, level, me).wait_recv()
                tb[g, 2, :, rows, :] = (
                    tb[g, 2, :, rows, :].astype(f32) + cr[g, level, :, rows, :].astype(f32)
                ).astype(bf16)

        @pl.when((col >= 2) & (row >= 1))
        def _():
            term_home(i, 2, me - 4).start()

    arrivals = (
        (0, (col <= 2) & (me + 1 < DEVICES)),
        (1, col <= 1),
        (2, me + 4 < DEVICES),
        (3, me + 8 < DEVICES),
    )

    def finish(g):
        for level, cond in arrivals:
            @pl.when(cond)
            def _():
                term_home(2 * g, level, me).wait_recv()
                term_home(2 * g + 1, level, me).wait_recv()
                own[g] = own[g] + rb[g, level].astype(f32)

        def extra(i, _):
            @pl.when(me + gap_of(i) < DEVICES)
            def _():
                extra_term(g, i, me).wait_recv()
            return 0

        lax.fori_loop(0, len(FAR), extra, 0)
        for part, ref in enumerate((dk, dv)):
            folded = dot(spread[...], xr[2 * g + part], TN)
            ref[:, lanes(g)] = (jnp.transpose(own[g, part]) + folded).astype(bf16)

    lane = lax.broadcasted_iota(jnp.int32, (BLOCK, PAIR), 1)
    factor = math.log2(math.e) / math.sqrt(HD)
    scaling = 1.0 / math.sqrt(HD)

    def keys_of(g, c, part):
        if c == 0:
            return (k, v)[part][:, lanes(g)]
        if c < 5:
            return rx[g, c - 1, part]
        return xx[g, part]

    def features_of(head):
        return pl.ds(pl.multiple_of(head * HD, HD), HD)

    def only(head, array):
        return jnp.where((lane // HD) == head, array, jnp.zeros_like(array))

    def folded_lanes(array, op):
        result = array[:, :PAIR]
        for x in range(1, array.shape[1] // PAIR):
            result = op(result, array[:, x * PAIR:(x + 1) * PAIR])
        return result

    def attend(g, query, c):
        low, size = CHUNKS[c]
        scores = dot(query, keys_of(g, c, 0), NT) * factor
        if c == 0:
            r = lax.broadcasted_iota(jnp.int32, (BLOCK, BLOCK), 0)
            j = lax.broadcasted_iota(jnp.int32, (BLOCK, BLOCK), 1)
            scores = jnp.where(r >= j, scores, very_negative)
        else:
            scores = scores + bias[0:1, low:low + size]
        top = jnp.max(folded_lanes(scores, jnp.maximum), axis=1, keepdims=True)
        weights = jnp.exp2(scores - top)
        total = jnp.sum(folded_lanes(weights, jnp.add), axis=1, keepdims=True)
        weights = weights.astype(bf16)
        return top, weights, total, dot(weights, keys_of(g, c, 1), NN)

    def own_forward(i, _):
        g, head = i // 2, i % 2
        top, weights, total, mixed = attend(g, only(head, q[:, lanes(g)]), 0)
        p_own[i] = weights
        o_own[i] = mixed
        stats[i] = jnp.where(lane == 0, top, total)
        return 0

    def forward(g, head):
        i = 2 * g + head
        query = only(head, q[:, lanes(g)])
        tops, totals, mixes_ = [stats[i, :, 0:1]], [stats[i, :, 1:2]], [o_own[i]]
        for c in range(1, 6):
            low, size = CHUNKS[c]
            top, weights, total, mixed = attend(g, query, c)
            p_far[:, low - BLOCK:low - BLOCK + size] = weights
            tops.append(top)
            totals.append(total)
            mixes_.append(mixed)
        top = tops[0]
        for c in range(1, 6):
            top = jnp.maximum(top, tops[c])
        shares = [jnp.exp2(x - top) for x in tops]
        total = shares[0] * totals[0]
        for c in range(1, 6):
            total = total + shares[c] * totals[c]
        total = 1.0 / total
        shares = [share * total for share in shares]
        mixed = mixes_[0] * shares[0]
        for c in range(1, 6):
            mixed = mixed + mixes_[c] * shares[c]
        mixed = mixed.astype(bf16)
        grad = only(head, do[:, lanes(g)]).astype(f32)
        delta = jnp.sum(grad * mixed.astype(f32), axis=1, keepdims=True)
        o[:, lanes(g)] = jnp.where((lane // HD) == head, mixed, o[:, lanes(g)])
        columns = jnp.where(lane == 6, delta, 0.0)
        for c in range(6):
            columns = jnp.where(lane == c, shares[c], columns)
        stats[i] = columns
        share_rows[i] = jnp.transpose(columns)[0:8, :]

    def differentiate(g, head, c, grad, columns, weights):
        i = 2 * g + head
        share = columns[:, c:c + 1]
        keys = keys_of(g, c, 0)
        scaled = (grad * share).astype(bf16)
        scaled_t = (dt[g, features_of(head), :].astype(f32) * share_rows[i, c:c + 1, :]).astype(bf16)
        weight_grads = dot(scaled, keys_of(g, c, 1), NT)
        score_grads = (weights.astype(f32) * (weight_grads - columns[:, 6:7] * share)).astype(bf16)
        half = BLOCK // 2
        query_grad = jnp.concatenate(
            [dot(score_grads[:half], keys, NN), dot(score_grads[half:], keys, NN)], axis=0
        )
        key_term = dot(qt[g, features_of(head), :], score_grads, NN) * scaling
        return query_grad, key_term, dot(scaled_t, weights, NN)

    def backward(g, head):
        i = 2 * g + head
        grad = only(head, do[:, lanes(g)]).astype(f32)
        columns = stats[i]
        features = features_of(head)
        query_grad = jnp.zeros((BLOCK, PAIR), f32)
        for c in range(1, 6):
            low, size = CHUNKS[c]
            part_grad, *terms = differentiate(
                g, head, c, grad, columns, p_far[:, low - BLOCK:low - BLOCK + size]
            )
            query_grad = query_grad + part_grad
            for part, term in enumerate(terms):
                if c < 5:
                    tb[g, c - 1, part, features, :] = term.astype(bf16)
                else:
                    et[part, features, :] = term
        o_own[i] = query_grad

    def own_backward(i, _):
        g, head = i // 2, i % 2
        grad = only(head, do[:, lanes(g)]).astype(f32)
        part_grad, *terms = differentiate(g, head, 0, grad, stats[i], p_own[i])
        for part, term in enumerate(terms):
            own[g, part, features_of(head), :] = term
        query_grad = ((o_own[i] + part_grad) * scaling).astype(bf16)
        dq[:, lanes(g)] = jnp.where((lane // HD) == head, query_grad, dq[:, lanes(g)])
        return 0

    def transposed(a):
        return jnp.transpose(a.astype(f32)).astype(bf16)

    for g in range(GROUPS):
        qt[g] = transposed(q[:, g * PAIR:(g + 1) * PAIR])
        dt[g] = transposed(do[:, g * PAIR:(g + 1) * PAIR])
    o[...] = jnp.zeros_like(o)
    dq[...] = jnp.zeros_like(dq)

    def own_forwards(g, _):
        own_forward(2 * g, 0)
        own_forward(2 * g + 1, 0)
        return 0

    lax.fori_loop(0, GROUPS // 2, own_forwards, 0)
    relay_part(0, 1)
    send_both(0, (farthest,))
    send_extras(0)
    lax.fori_loop(GROUPS // 2, GROUPS, own_forwards, 0)
    send_both(1, relayed)

    def wait_extras(g):
        def one(i, _):
            @pl.when(me - gap_of(i) >= 0)
            def _():
                extra_copy(g, i, me).wait_recv()
            return 0

        lax.fori_loop(0, len(FAR), one, 0)

    def step(i, _):
        g = i // 2
        head = i % 2

        @pl.when(head == 0)
        def _():
            for level in (0, 1, 3):
                wait_blocks(g, level)
            wait_extras(g)

        @pl.when((head == 0) & (g + 1 < GROUPS))
        def _():
            send_both(g + 1, nearest)
            relay_blocks(g + 1)
            send_both(g + 1, (farthest,))
            send_extras(g + 1)

        forward(g, head)

        @pl.when((head == 1) & (g + 2 < GROUPS))
        def _():
            send_both(g + 2, relayed)

        backward(g, head)

        @pl.when(i >= LAG)
        def _():
            mix_terms(i - LAG)

        send_terms(i)

        @pl.when(head == 1)
        def _():
            send_extra_terms(g)

        return 0

    lax.fori_loop(0, 2 * GROUPS, step, 0)

    def own_backwards(g, _):
        own_backward(2 * g, 0)
        own_backward(2 * g + 1, 0)
        return 0

    lax.fori_loop(0, GROUPS // 2, own_backwards, 0)

    def late_mix(i, _):
        mix_terms(i)
        return 0

    lax.fori_loop(2 * GROUPS - LAG, 2 * GROUPS, late_mix, 0)
    lax.fori_loop(GROUPS // 2, GROUPS, own_backwards, 0)

    def last(g, _):
        finish(g)
        return 0

    lax.fori_loop(0, GROUPS, last, 0)

    def left(g, _):
        for level, cond in direct + (farthest,):
            @pl.when(cond)
            def _():
                for copy in own_copies(g, level, me):
                    copy.wait_send()
        for level, back, cond in relays:
            @pl.when(cond)
            def _():
                for copy in relay_copies(g, level, me):
                    copy.wait_send()
        for level, distance in enumerate(DISTANCES):
            @pl.when(me >= distance)
            def _():
                term_home(2 * g, level, me).wait_send()
                term_home(2 * g + 1, level, me).wait_send()

        def extra(i, _):
            @pl.when(me + gap_of(i) < DEVICES)
            def _():
                extra_copy(g, i, me).wait_send()

            @pl.when(me - gap_of(i) >= 0)
            def _():
                extra_term(g, i, me).wait_send()
            return 0

        lax.fori_loop(0, len(FAR), extra, 0)
        return 0

    lax.fori_loop(0, GROUPS, left, 0)


def publish(*refs):
    for i in range(4):
        refs[i + 4][...] = refs[i][...]


def local(queries, key_rows, value_rows, grad_output, extra_blocks):
    whole = pl.BlockSpec(memory_space=pltpu.VMEM)
    slots = len(FAR)
    results = pl.pallas_call(
        kernel,
        out_shape=[jax.ShapeDtypeStruct((BLOCK, WIDTH), bf16)] * 4,
        in_specs=[whole] * 4 + [pl.BlockSpec(memory_space=pltpu.SMEM)],
        out_specs=[whole] * 4,
        scratch_shapes=[
            pltpu.VMEM((GROUPS, 4, 2, BLOCK, PAIR), bf16),
            pltpu.VMEM((GROUPS, 2, EXTRA_ROWS, PAIR), bf16),
            pltpu.VMEM((GROUPS, 2, EXTRA_ROWS, PAIR), bf16),
            pltpu.VMEM((GROUPS, 4, 2, PAIR, BLOCK), bf16),
            pltpu.VMEM((GROUPS, 2, PAIR, BLOCK), f32),
            pltpu.VMEM((2, PAIR, EXTRA_ROWS), f32),
            pltpu.VMEM((2 * GROUPS, EXTRA_ROWS, PAIR), bf16),
            pltpu.VMEM((GROUPS, 4, 2, PAIR, BLOCK), bf16),
            pltpu.VMEM((GROUPS, 2, 2, PAIR, BLOCK), bf16),
            pltpu.VMEM((2 * GROUPS, EXTRA_ROWS, PAIR), bf16),
            pltpu.VMEM((BLOCK, KEYS - BLOCK), bf16),
            pltpu.VMEM((2 * GROUPS, BLOCK, BLOCK), bf16),
            pltpu.VMEM((2 * GROUPS, BLOCK, PAIR), f32),
            pltpu.VMEM((2 * GROUPS, BLOCK, PAIR), f32),
            pltpu.VMEM((2 * GROUPS, 8, BLOCK), f32),
            pltpu.VMEM((GROUPS, PAIR, BLOCK), bf16),
            pltpu.VMEM((GROUPS, PAIR, BLOCK), bf16),
            pltpu.VMEM((8, KEYS), f32),
            pltpu.VMEM((EXTRA_ROWS, BLOCK), bf16),
            pltpu.SemaphoreType.DMA((GROUPS, 4, 2)),
            pltpu.SemaphoreType.DMA((GROUPS, 4, 2)),
            pltpu.SemaphoreType.DMA((GROUPS, 4, 2)),
            pltpu.SemaphoreType.DMA((GROUPS, slots)),
            pltpu.SemaphoreType.DMA((GROUPS, slots)),
            pltpu.SemaphoreType.DMA((2 * GROUPS, 4)),
            pltpu.SemaphoreType.DMA((2 * GROUPS, 4)),
            pltpu.SemaphoreType.DMA((2 * GROUPS, 4)),
            pltpu.SemaphoreType.DMA((GROUPS, slots)),
            pltpu.SemaphoreType.DMA((GROUPS, slots)),
        ],
        compiler_params=pltpu.CompilerParams(
            collective_id=0, has_side_effects=True, vmem_limit_bytes=60 << 20
        ),
    )(queries, key_rows, value_rows, grad_output, extra_blocks)
    return pl.pallas_call(
        publish,
        out_shape=[jax.ShapeDtypeStruct((BLOCK, WIDTH), bf16)] * 4,
        in_specs=[whole] * 4,
        out_specs=[whole] * 4,
    )(*results)


def solution(mesh):
    rows = P(("member", "tm"), None)
    return jax.shard_map(
        local,
        mesh=mesh,
        in_specs=(rows, rows, rows, rows, P("member", None)),
        out_specs=(rows, rows, rows, rows),
        check_vma=False,
    )
```

```python
import math

import jax
import jax.numpy as jnp
from jax import lax
from jax.experimental import pallas as pl
from jax.experimental.pallas import tpu as pltpu
from jax.sharding import PartitionSpec as P

HD = 64
SUB = 16
CAP = 2
MESH = pl.DeviceIdType.MESH
NT = (((1,), (1,)), ((), ()))
NN = (((1,), (0,)), ((), ()))
TN = (((0,), (0,)), ((), ()))
very_negative = -1e30
f32 = jnp.float32
bf16 = jnp.bfloat16

DEVICES = 16
SIDE = 4
BLOCK = 512
WIDTH = 512
PAIR = 128
GROUPS = WIDTH // PAIR
PER_BLOCK = BLOCK // SUB
DISTANCES = (1, 2, 4, 8)
FAR = tuple(d for d in range(1, DEVICES) if d not in DISTANCES)
SLOT_ROWS = CAP * SUB
LAG = 2
EXTRA_ROWS = 384
KEYS = 5 * BLOCK + EXTRA_ROWS
CHUNKS = tuple((i * BLOCK, BLOCK) for i in range(5)) + ((5 * BLOCK, EXTRA_ROWS),)


def dot(a, b, dims):
    return lax.dot_general(a, b, dims, preferred_element_type=f32)


def kernel(
    q, k, v, do, table,
    o, dq, dk, dv,
    rx, xx, xs, tb, own, et, xt, rb, cr, xr,
    p_far, p_own, o_own, stats, share_rows, qt, dt, bias, spread,
    send_kv, recv_kv, send_relay, send_x, recv_x,
    send_t, recv_t, recv_c, send_xt, recv_xt,
):
    me = lax.axis_index("tm")
    col = lax.rem(me, SIDE)
    row = me // SIDE

    def device(index):
        return {"tm": index}

    barrier = pltpu.get_barrier_semaphore()
    for i in range(DEVICES):
        @pl.when(me != i)
        def _():
            pl.semaphore_signal(barrier, inc=1, device_id=device(i), device_id_type=MESH)
    pl.semaphore_wait(barrier, DEVICES - 1)

    def lanes(g):
        return pl.ds(pl.multiple_of(g * PAIR, PAIR), PAIR)

    def kv_copies(g, level, src_k, src_v, send, to):
        return [
            pltpu.make_async_remote_copy(
                src_ref=src,
                dst_ref=rx.at[g, level, part],
                send_sem=send.at[g, level, part],
                recv_sem=recv_kv.at[g, level, part],
                device_id=device(to),
                device_id_type=MESH,
            )
            for part, src in enumerate((src_k, src_v))
        ]

    def own_copies(g, level, to):
        return kv_copies(g, level, k.at[:, lanes(g)], v.at[:, lanes(g)], send_kv, to)

    def relay_copies(g, level, to):
        return kv_copies(g, level, rx.at[g, 2, 0], rx.at[g, 2, 1], send_relay, to)

    relayed = ((2, me + 4 < DEVICES),)
    nearest = (
        (0, (col < 3) & (me + 1 < DEVICES)),
        (1, col < 2),
    )
    direct = relayed + nearest
    farthest = (3, me + 8 < DEVICES)
    relays = (
        (0, 3, (col == 3) & (row >= 1)),
        (1, 2, (col >= 2) & (row >= 1)),
    )

    def send_part(g, part, targets):
        for level, cond in targets:
            @pl.when(cond)
            def _():
                own_copies(g, level, me + DISTANCES[level])[part].start()

    def send_both(g, targets):
        for part in range(2):
            send_part(g, part, targets)

    def wait_part(g, level, part):
        @pl.when(me >= DISTANCES[level])
        def _():
            own_copies(g, level, me)[part].wait_recv()

    def wait_blocks(g, level):
        for part in range(2):
            wait_part(g, level, part)

    def relay_part(g, part):
        wait_part(g, 2, part)
        for level, back, cond in relays:
            @pl.when(cond)
            def _():
                relay_copies(g, level, me - back)[part].start()

    def relay_blocks(g):
        for part in range(2):
            relay_part(g, part)

    send_part(0, 0, direct)

    def gap_of(i):
        return i + 3 + (i + 10) // 11 + (i + 7) // 11

    def extra_copy(g, i, to):
        rows = pl.ds(pl.multiple_of(i * SLOT_ROWS, SLOT_ROWS), SLOT_ROWS)
        return pltpu.make_async_remote_copy(
            src_ref=xs.at[g, :, rows, :],
            dst_ref=xx.at[g, :, rows, :],
            send_sem=send_x.at[g, i],
            recv_sem=recv_x.at[g, i],
            device_id=device(to),
            device_id_type=MESH,
        )

    spread[...] = jnp.zeros_like(spread)

    def find(i, _):
        other = me + gap_of(i)

        @pl.when(other < DEVICES)
        def _():
            first = me * PER_BLOCK
            count = jnp.int32(0)
            index = [jnp.int32(0), jnp.int32(0)]
            for n in range(table.shape[1]):
                entry = table[other, n]
                inside = entry - first
                mine = (inside >= 0) & (inside < PER_BLOCK)
                for slot in range(CAP):
                    index[slot] = jnp.where(mine & (count == slot), inside, index[slot])
                count = count + jnp.where(mine, 1, 0)
            for slot in range(CAP):
                base = jnp.where(count > slot, index[slot] * SUB, jnp.int32(-4096))
                hit = lax.broadcasted_iota(jnp.int32, (SUB, BLOCK), 1) == (
                    lax.broadcasted_iota(jnp.int32, (SUB, BLOCK), 0) + base
                )
                spread[pl.ds(pl.multiple_of(i * SLOT_ROWS + slot * SUB, SUB), SUB), :] = jnp.where(
                    hit, 1.0, 0.0
                ).astype(bf16)

        return 0

    lax.fori_loop(0, len(FAR), find, 0)
    for part, ref in enumerate((k, v)):
        for g in range(GROUPS):
            xs[g, part] = dot(spread[...], ref[:, g * PAIR:(g + 1) * PAIR], NN).astype(bf16)

    def send_extras(g):
        def one(i, _):
            @pl.when(me + gap_of(i) < DEVICES)
            def _():
                extra_copy(g, i, me + gap_of(i)).start()
            return 0

        lax.fori_loop(0, len(FAR), one, 0)

    relay_part(0, 0)
    send_part(0, 1, direct)

    key_row = lax.broadcasted_iota(jnp.int32, (8, BLOCK), 1)
    for level, distance in enumerate(DISTANCES):
        sub_block = (me - distance) * PER_BLOCK + (key_row >> 4)
        times = jnp.zeros((8, BLOCK), f32)
        for n in range(table.shape[1]):
            times = times + jnp.where(sub_block == table[me, n], 1.0, 0.0)
        value = jnp.where(times > 0.5, 1.0, 0.0)
        low, size = CHUNKS[1 + level]
        bias[:, low:low + size] = jnp.where(sub_block >= 0, value, very_negative)
    key_row = lax.broadcasted_iota(jnp.int32, (8, EXTRA_ROWS), 1)
    place = key_row >> 5
    owner = me - (place + 3 + jnp.where(place >= 1, 1, 0) + jnp.where(place >= 4, 1, 0))
    times = jnp.zeros((8, EXTRA_ROWS), f32)
    for n in range(table.shape[1]):
        entry = table[me, n]
        inside = entry - owner * PER_BLOCK
        times = times + jnp.where((inside >= 0) & (inside < PER_BLOCK), 1.0, 0.0)
    slot_of = ((key_row >> 4) & 1).astype(f32)
    live = (times > slot_of + 0.5) & (owner >= 0) & (place < len(FAR))
    bias[:, 5 * BLOCK:] = jnp.where(live, 0.0, very_negative)

    for level, distance in enumerate(DISTANCES):
        @pl.when(me < distance)
        def _():
            def clear(g, _):
                rx[g, level] = jnp.zeros(rx.shape[2:], bf16)
                return 0
            lax.fori_loop(0, GROUPS, clear, 0)
    tail = len(FAR) * SLOT_ROWS
    xx[:, :, tail:, :] = jnp.zeros((GROUPS, 2, EXTRA_ROWS - tail, PAIR), bf16)
    xr[:, tail:, :] = jnp.zeros((2 * GROUPS, EXTRA_ROWS - tail, PAIR), bf16)

    def clear_extra(i, _):
        rows = pl.ds(pl.multiple_of(i * SLOT_ROWS, SLOT_ROWS), SLOT_ROWS)

        @pl.when(me - gap_of(i) < 0)
        def _():
            xx[:, :, rows, :] = jnp.zeros((GROUPS, 2, SLOT_ROWS, PAIR), bf16)

        @pl.when(me + gap_of(i) >= DEVICES)
        def _():
            xr[:, rows, :] = jnp.zeros((2 * GROUPS, SLOT_ROWS, PAIR), bf16)

        return 0

    lax.fori_loop(0, len(FAR), clear_extra, 0)

    def term_rows(i):
        return i // 2, pl.ds(pl.multiple_of((i % 2) * HD, HD), HD)

    def term_copy(i, level, place, recv, to):
        g, rows = term_rows(i)
        return pltpu.make_async_remote_copy(
            src_ref=tb.at[g, level, :, rows, :],
            dst_ref=place.at[g, level, :, rows, :],
            send_sem=send_t.at[i, level],
            recv_sem=recv.at[i, level],
            device_id=device(to),
            device_id_type=MESH,
        )

    def term_home(i, level, to):
        return term_copy(i, level, rb, recv_t, to)

    def term_aside(i, level, to):
        return term_copy(i, level, cr, recv_c, to)

    def extra_term(g, i, to):
        rows = pl.ds(pl.multiple_of(i * SLOT_ROWS, SLOT_ROWS), SLOT_ROWS)
        both = pl.ds(2 * g, 2)
        return pltpu.make_async_remote_copy(
            src_ref=xt.at[both, rows, :],
            dst_ref=xr.at[both, rows, :],
            send_sem=send_xt.at[g, i],
            recv_sem=recv_xt.at[g, i],
            device_id=device(to),
            device_id_type=MESH,
        )

    homes = (
        (0, col >= 1),
        (1, col >= 2),
        (3, me >= 8),
        (2, (col < 2) & (row >= 1)),
    )
    asides = (
        (0, 3, (col == 0) & (row >= 1)),
        (1, 2, (col < 2) & (row >= 1)),
    )
    mixes = (
        (0, (col == 3) & (row >= 1)),
        (1, (col >= 2) & (row >= 1)),
    )

    def send_terms(i):
        for level, ahead, cond in asides:
            @pl.when(cond)
            def _():
                term_aside(i, level, me + ahead).start()
        send_homes(i, (0, 1))

    def send_homes(i, levels):
        for level, cond in homes:
            if level in levels:
                @pl.when(cond & (me >= DISTANCES[level]))
                def _():
                    term_home(i, level, me - DISTANCES[level]).start()

    def send_extra_terms(g):
        for part in range(2):
            xt[2 * g + part] = jnp.transpose(et[part]).astype(bf16)

        def extra(i, _):
            @pl.when(me - gap_of(i) >= 0)
            def _():
                extra_term(g, i, me - gap_of(i)).start()
            return 0

        lax.fori_loop(0, len(FAR), extra, 0)

    def mix_terms(i):
        g, rows = term_rows(i)
        for level, cond in mixes:
            @pl.when(cond)
            def _():
                term_aside(i, level, me).wait_recv()
                tb[g, 2, :, rows, :] = (
                    tb[g, 2, :, rows, :].astype(f32) + cr[g, level, :, rows, :].astype(f32)
                ).astype(bf16)

        @pl.when((col >= 2) & (row >= 1))
        def _():
            term_home(i, 2, me - 4).start()

    arrivals = (
        (0, (col <= 2) & (me + 1 < DEVICES)),
        (1, col <= 1),
        (2, me + 4 < DEVICES),
        (3, me + 8 < DEVICES),
    )

    def finish(g):
        for level, cond in arrivals:
            @pl.when(cond)
            def _():
                term_home(2 * g, level, me).wait_recv()
                term_home(2 * g + 1, level, me).wait_recv()
                own[g] = own[g] + rb[g, level].astype(f32)

        def extra(i, _):
            @pl.when(me + gap_of(i) < DEVICES)
            def _():
                extra_term(g, i, me).wait_recv()
            return 0

        lax.fori_loop(0, len(FAR), extra, 0)
        for part, ref in enumerate((dk, dv)):
            folded = dot(spread[...], xr[2 * g + part], TN)
            ref[:, lanes(g)] = (jnp.transpose(own[g, part]) + folded).astype(bf16)

    lane = lax.broadcasted_iota(jnp.int32, (BLOCK, PAIR), 1)
    factor = math.log2(math.e) / math.sqrt(HD)
    scaling = 1.0 / math.sqrt(HD)

    def keys_of(g, c, part):
        if c == 0:
            return (k, v)[part][:, lanes(g)]
        if c < 5:
            return rx[g, c - 1, part]
        return xx[g, part]

    def features_of(head):
        return pl.ds(pl.multiple_of(head * HD, HD), HD)

    def only(head, array):
        return jnp.where((lane // HD) == head, array, jnp.zeros_like(array))

    def folded_lanes(array, op):
        result = array[:, :PAIR]
        for x in range(1, array.shape[1] // PAIR):
            result = op(result, array[:, x * PAIR:(x + 1) * PAIR])
        return result

    def attend(g, query, c):
        low, size = CHUNKS[c]
        scores = dot(query, keys_of(g, c, 0), NT) * factor
        if c == 0:
            r = lax.broadcasted_iota(jnp.int32, (BLOCK, BLOCK), 0)
            j = lax.broadcasted_iota(jnp.int32, (BLOCK, BLOCK), 1)
            scores = jnp.where(r >= j, scores, very_negative)
        else:
            scores = scores + bias[0:1, low:low + size]
        top = jnp.max(folded_lanes(scores, jnp.maximum), axis=1, keepdims=True)
        weights = jnp.exp2(scores - top)
        total = jnp.sum(folded_lanes(weights, jnp.add), axis=1, keepdims=True)
        weights = weights.astype(bf16)
        return top, weights, total, dot(weights, keys_of(g, c, 1), NN)

    def own_forward(i, _):
        g, head = i // 2, i % 2
        top, weights, total, mixed = attend(g, only(head, q[:, lanes(g)]), 0)
        p_own[i] = weights
        o_own[i] = mixed
        stats[i] = jnp.where(lane == 0, top, total)
        return 0

    def forward(g, head):
        i = 2 * g + head
        query = only(head, q[:, lanes(g)])
        tops, totals, mixes_ = [stats[i, :, 0:1]], [stats[i, :, 1:2]], [o_own[i]]
        for c in range(1, 6):
            low, size = CHUNKS[c]
            top, weights, total, mixed = attend(g, query, c)
            p_far[:, low - BLOCK:low - BLOCK + size] = weights
            tops.append(top)
            totals.append(total)
            mixes_.append(mixed)
        top = tops[0]
        for c in range(1, 6):
            top = jnp.maximum(top, tops[c])
        shares = [jnp.exp2(x - top) for x in tops]
        total = shares[0] * totals[0]
        for c in range(1, 6):
            total = total + shares[c] * totals[c]
        total = 1.0 / total
        shares = [share * total for share in shares]
        mixed = mixes_[0] * shares[0]
        for c in range(1, 6):
            mixed = mixed + mixes_[c] * shares[c]
        mixed = mixed.astype(bf16)
        grad = only(head, do[:, lanes(g)]).astype(f32)
        delta = jnp.sum(grad * mixed.astype(f32), axis=1, keepdims=True)
        o[:, lanes(g)] = jnp.where((lane // HD) == head, mixed, o[:, lanes(g)])
        columns = jnp.where(lane == 6, delta, 0.0)
        for c in range(6):
            columns = jnp.where(lane == c, shares[c], columns)
        stats[i] = columns
        share_rows[i] = jnp.transpose(columns)[0:8, :]

    def differentiate(g, head, c, grad, columns, weights):
        i = 2 * g + head
        share = columns[:, c:c + 1]
        keys = keys_of(g, c, 0)
        scaled = (grad * share).astype(bf16)
        scaled_t = (dt[g, features_of(head), :].astype(f32) * share_rows[i, c:c + 1, :]).astype(bf16)
        weight_grads = dot(scaled, keys_of(g, c, 1), NT)
        score_grads = (weights.astype(f32) * (weight_grads - columns[:, 6:7] * share)).astype(bf16)
        half = BLOCK // 2
        query_grad = jnp.concatenate(
            [dot(score_grads[:half], keys, NN), dot(score_grads[half:], keys, NN)], axis=0
        )
        key_term = dot(qt[g, features_of(head), :], score_grads, NN) * scaling
        return query_grad, key_term, dot(scaled_t, weights, NN)

    def backward(g, head):
        i = 2 * g + head
        grad = only(head, do[:, lanes(g)]).astype(f32)
        columns = stats[i]
        features = features_of(head)
        query_grad = jnp.zeros((BLOCK, PAIR), f32)
        for c in range(1, 6):
            low, size = CHUNKS[c]
            part_grad, *terms = differentiate(
                g, head, c, grad, columns, p_far[:, low - BLOCK:low - BLOCK + size]
            )
            query_grad = query_grad + part_grad
            for part, term in enumerate(terms):
                if c < 5:
                    tb[g, c - 1, part, features, :] = term.astype(bf16)
                else:
                    et[part, features, :] = term
            if c == 2:
                send_terms(i)
        o_own[i] = query_grad

    def own_backward(i, _):
        g, head = i // 2, i % 2
        grad = only(head, do[:, lanes(g)]).astype(f32)
        part_grad, *terms = differentiate(g, head, 0, grad, stats[i], p_own[i])
        for part, term in enumerate(terms):
            own[g, part, features_of(head), :] = term
        query_grad = ((o_own[i] + part_grad) * scaling).astype(bf16)
        dq[:, lanes(g)] = jnp.where((lane // HD) == head, query_grad, dq[:, lanes(g)])
        return 0

    def transposed(a):
        return jnp.transpose(a.astype(f32)).astype(bf16)

    for g in range(GROUPS):
        qt[g] = transposed(q[:, g * PAIR:(g + 1) * PAIR])
        dt[g] = transposed(do[:, g * PAIR:(g + 1) * PAIR])
    o[...] = jnp.zeros_like(o)
    dq[...] = jnp.zeros_like(dq)

    def own_forwards(g, _):
        own_forward(2 * g, 0)
        own_forward(2 * g + 1, 0)
        return 0

    lax.fori_loop(0, GROUPS // 2, own_forwards, 0)
    relay_part(0, 1)
    send_both(0, (farthest,))
    send_extras(0)
    lax.fori_loop(GROUPS // 2, GROUPS, own_forwards, 0)
    send_both(1, relayed)

    def wait_extras(g):
        def one(i, _):
            @pl.when(me - gap_of(i) >= 0)
            def _():
                extra_copy(g, i, me).wait_recv()
            return 0

        lax.fori_loop(0, len(FAR), one, 0)

    def step(i, _):
        g = i // 2
        head = i % 2

        @pl.when(i >= LAG)
        def _():
            own_backward(i - LAG, 0)

        @pl.when(head == 0)
        def _():
            for level in (0, 1, 3):
                wait_blocks(g, level)
            wait_extras(g)

        @pl.when((head == 0) & (g + 1 < GROUPS))
        def _():
            send_both(g + 1, nearest)
            send_extras(g + 1)
            relay_blocks(g + 1)
            send_both(g + 1, (farthest,))

        forward(g, head)

        @pl.when((head == 1) & (g + 2 < GROUPS))
        def _():
            send_both(g + 2, relayed)

        backward(g, head)

        @pl.when(i >= LAG)
        def _():
            mix_terms(i - LAG)

        send_homes(i, (2, 3))

        @pl.when(head == 1)
        def _():
            send_extra_terms(g)

        return 0

    lax.fori_loop(0, 2 * GROUPS, step, 0)

    def ending(i, _):
        mix_terms(i)
        own_backward(i, 0)
        return 0

    lax.fori_loop(2 * GROUPS - LAG, 2 * GROUPS, ending, 0)

    def last(g, _):
        finish(g)
        return 0

    lax.fori_loop(0, GROUPS, last, 0)

    def left(g, _):
        for level, cond in direct + (farthest,):
            @pl.when(cond)
            def _():
                for copy in own_copies(g, level, me):
                    copy.wait_send()
        for level, back, cond in relays:
            @pl.when(cond)
            def _():
                for copy in relay_copies(g, level, me):
                    copy.wait_send()
        for level, distance in enumerate(DISTANCES):
            @pl.when(me >= distance)
            def _():
                term_home(2 * g, level, me).wait_send()
                term_home(2 * g + 1, level, me).wait_send()

        def extra(i, _):
            @pl.when(me + gap_of(i) < DEVICES)
            def _():
                extra_copy(g, i, me).wait_send()

            @pl.when(me - gap_of(i) >= 0)
            def _():
                extra_term(g, i, me).wait_send()
            return 0

        lax.fori_loop(0, len(FAR), extra, 0)
        return 0

    lax.fori_loop(0, GROUPS, left, 0)


def publish(*refs):
    for i in range(4):
        refs[i + 4][...] = refs[i][...]


def local(queries, key_rows, value_rows, grad_output, extra_blocks):
    whole = pl.BlockSpec(memory_space=pltpu.VMEM)
    slots = len(FAR)
    results = pl.pallas_call(
        kernel,
        out_shape=[jax.ShapeDtypeStruct((BLOCK, WIDTH), bf16)] * 4,
        in_specs=[whole] * 4 + [pl.BlockSpec(memory_space=pltpu.SMEM)],
        out_specs=[whole] * 4,
        scratch_shapes=[
            pltpu.VMEM((GROUPS, 4, 2, BLOCK, PAIR), bf16),
            pltpu.VMEM((GROUPS, 2, EXTRA_ROWS, PAIR), bf16),
            pltpu.VMEM((GROUPS, 2, EXTRA_ROWS, PAIR), bf16),
            pltpu.VMEM((GROUPS, 4, 2, PAIR, BLOCK), bf16),
            pltpu.VMEM((GROUPS, 2, PAIR, BLOCK), f32),
            pltpu.VMEM((2, PAIR, EXTRA_ROWS), f32),
            pltpu.VMEM((2 * GROUPS, EXTRA_ROWS, PAIR), bf16),
            pltpu.VMEM((GROUPS, 4, 2, PAIR, BLOCK), bf16),
            pltpu.VMEM((GROUPS, 2, 2, PAIR, BLOCK), bf16),
            pltpu.VMEM((2 * GROUPS, EXTRA_ROWS, PAIR), bf16),
            pltpu.VMEM((BLOCK, KEYS - BLOCK), bf16),
            pltpu.VMEM((2 * GROUPS, BLOCK, BLOCK), bf16),
            pltpu.VMEM((2 * GROUPS, BLOCK, PAIR), f32),
            pltpu.VMEM((2 * GROUPS, BLOCK, PAIR), f32),
            pltpu.VMEM((2 * GROUPS, 8, BLOCK), f32),
            pltpu.VMEM((GROUPS, PAIR, BLOCK), bf16),
            pltpu.VMEM((GROUPS, PAIR, BLOCK), bf16),
            pltpu.VMEM((8, KEYS), f32),
            pltpu.VMEM((EXTRA_ROWS, BLOCK), bf16),
            pltpu.SemaphoreType.DMA((GROUPS, 4, 2)),
            pltpu.SemaphoreType.DMA((GROUPS, 4, 2)),
            pltpu.SemaphoreType.DMA((GROUPS, 4, 2)),
            pltpu.SemaphoreType.DMA((GROUPS, slots)),
            pltpu.SemaphoreType.DMA((GROUPS, slots)),
            pltpu.SemaphoreType.DMA((2 * GROUPS, 4)),
            pltpu.SemaphoreType.DMA((2 * GROUPS, 4)),
            pltpu.SemaphoreType.DMA((2 * GROUPS, 4)),
            pltpu.SemaphoreType.DMA((GROUPS, slots)),
            pltpu.SemaphoreType.DMA((GROUPS, slots)),
        ],
        compiler_params=pltpu.CompilerParams(
            collective_id=0, has_side_effects=True, vmem_limit_bytes=60 << 20
        ),
    )(queries, key_rows, value_rows, grad_output, extra_blocks)
    return pl.pallas_call(
        publish,
        out_shape=[jax.ShapeDtypeStruct((BLOCK, WIDTH), bf16)] * 4,
        in_specs=[whole] * 4,
        out_specs=[whole] * 4,
    )(*results)


def solution(mesh):
    rows = P(("member", "tm"), None)
    return jax.shard_map(
        local,
        mesh=mesh,
        in_specs=(rows, rows, rows, rows, P("member", None)),
        out_specs=(rows, rows, rows, rows),
        check_vma=False,
    )
```
